32 devices in a mesh: seq: 8 (over z, y), pipe: 4 (over x, core).
Axes of the slice: x: 2, y: 2, z: 4, core: 2. Of those that a mesh axis runs over, the one named last changes fastest.
Arguments:
- cotangent: bfloat16 [4, 4096, 4096], P('pipe', 'seq'), may hold values from -6 to 6
- input_map: bfloat16 [4, 4096, 128], P('pipe', 'seq'), may hold values from -0.30273438 to 0.30273438
- output_map: bfloat16 [4, 4096, 128], P('pipe', 'seq'), may hold values from -0.30273438 to 0.30273438
- log_decay: float32 [4, 4096, 32], P('pipe', 'seq'), may hold values from -2 to 0, as said below
- flight_starts: int32 [4, 4096], P('pipe', 'seq'), may hold values 0 or 1
- skip_gain: float32 [4, 32], P('pipe'), may hold values from 0.5 to 1.5
- in_weight: bfloat16 [4, 2048, 4096], P('pipe', 'seq'), may hold values from -0.09375 to 0.09375
Outputs:
- input_cotangent: bfloat16 [4, 4096, 2048], P('pipe', 'seq')
The draws below stay inside these ranges and needn't reach their ends.
Inputs may be any that keep to these rules, and one draw needn't show every extreme that they name: log_decay is never positive.
All inputs are finite; a program needn't handle non-finite values. No bound on the sum of `flight_starts` on one device may be relied on, other than what follows from the above.
Results may differ from the reference program's by a relative error of at most 0.009.
Values may be sent and summed in bfloat16 or wider, within the bound.
No kernel may reach another device: no remote copies, remote signals or barrier semaphores. Data moves between devices by JAX's collectives and lax.ppermute only.
A program may use at most 192 MiB of HBM per device.

```python
import math
import jax
import jax.numpy as jnp
from jax import lax

H = 32
P_SIZE = 128
N = 128
D = 2048
SPAN = 256
TOK_DEV = 512
TOKENS = 4096
N_PIPE = 4


def draw_log_decay(key, part):
    streams = jax.random.split(key, 7)
    slow_share = 0.5
    chosen = jax.random.uniform(streams[0], (N_PIPE, 1, H)) < slow_share
    slow = jnp.exp(jax.random.uniform(streams[1], (N_PIPE, 1, H), minval=math.log(0.03), maxval=math.log(0.3))) / TOKENS
    fast = jnp.exp(jax.random.uniform(streams[2], (N_PIPE, 1, H), minval=math.log(0.02), maxval=math.log(0.2)))
    forgetting_factors = jnp.where(chosen, slow, fast)
    approximate_guess = jax.random.uniform(streams[3], (N_PIPE, TOKENS, H), minval=0.6, maxval=1.6)
    portion_factor = jax.random.uniform(streams[4], (N_PIPE, TOKENS // TOK_DEV, 1, H), minval=0.6, maxval=1.6)
    portion_factor = jnp.broadcast_to(portion_factor, (N_PIPE, TOKENS // TOK_DEV, TOK_DEV, H)).reshape(N_PIPE, TOKENS, H)
    half = TOKENS // 2
    offsets = jax.random.randint(streams[5], (N_PIPE, 1, 2), 0, half)
    locator_numbers = offsets + jnp.array([0, half], jnp.int32)[None, None, :]
    objective_scores_list = jax.random.uniform(streams[6], (N_PIPE, 1, 2), minval=0.2, maxval=0.75)
    element_offset = jnp.arange(TOKENS)[None, :, None]
    spurt_extent = jnp.sum(jnp.where(element_offset == locator_numbers, jnp.log(1.0 - objective_scores_list), 0.0), axis=2, keepdims=True)
    return (-(forgetting_factors * approximate_guess * portion_factor) + spurt_extent).astype(jnp.float32)


def set_ends(result, stream_key, low, top_value):
    longest = result.shape.index(max(result.shape))
    spots = []
    for shift in (0, 1):
        where = [jax.random.randint(jax.random.fold_in(stream_key, axis), (), 0, length) for axis, length in enumerate(result.shape)]
        where[longest] = (where[longest] + shift) % result.shape[longest]
        spots.append(tuple(where))
    return result.at[spots[0]].set(low).at[spots[1]].set(top_value)


def steps_of(stream_key, shape, cuts, low, high):
    loudness = 1.0
    for position, parts in cuts:
        steps = jax.random.uniform(jax.random.fold_in(jax.random.fold_in(stream_key, 6), position), (parts,), jnp.float32, low / len(cuts), high / len(cuts))
        loudness = loudness * jnp.repeat(jnp.exp(steps), shape[position] // parts).reshape((-1,) + (1,) * (len(shape) - 1 - position))
    return loudness


def gaussian(stream_key, dims, deviation, reach, shards=(), held_as=jnp.bfloat16):
    values = deviation * jax.random.normal(stream_key, dims, jnp.float32)
    if shards:
        values = values * steps_of(stream_key, dims, shards, -0.22, 0.18)
    return jnp.clip(values, -reach, reach).astype(held_as)


def setup_inputs(seed: int = 0) -> dict:
    key_of = jax.random.split(jax.random.key(seed), 8)
    return {
        "cotangent": gaussian(key_of[0], (N_PIPE, TOKENS, H * P_SIZE), 1.0, 6.0, ((0, 4), (1, 8))),
        "input_map": gaussian(key_of[1], (N_PIPE, TOKENS, N), (0.17 * N ** -0.25), 0.30273438, ((0, 4), (1, 8))),
        "output_map": gaussian(key_of[2], (N_PIPE, TOKENS, N), (0.17 * N ** -0.25), 0.30273438, ((0, 4), (1, 8))),
        "log_decay": draw_log_decay(jax.random.fold_in(key_of[7], 71), 0),
        "flight_starts": set_ends((jax.random.randint(key_of[4], (N_PIPE, TOKENS), 0, TOKENS // 3) < 1).astype(jnp.int32), jax.random.fold_in(key_of[4], 1), 0, 1),
        "skip_gain": jnp.clip(0.5 + 1.0 * jax.random.uniform(key_of[5], (N_PIPE, H), jnp.float32) ** steps_of(key_of[5], (N_PIPE, H), ((0, 4),), -0.2, 0.2), 0.5, 1.5),
        "in_weight": gaussian(key_of[6], (N_PIPE, D, H * P_SIZE), (H * P_SIZE) ** -0.5, 0.09375, ((0, 4), (1, 8))),
    }


def block_grad(upstream, writes, reads, decays, marks, gains, later):
    running = jnp.cumsum(decays, axis=0)
    counts = jnp.cumsum(marks, axis=0).astype(jnp.int32)
    element_offset = jnp.arange(SPAN)
    upper = element_offset[:, None] <= element_offset[None, :]
    linked = upper & (counts[:, None] == counts[None, :])
    scores = jnp.dot(writes, reads.T, preferred_element_type=jnp.float32)
    spread = running.T[:, None, :] - running.T[:, :, None]
    weight = jnp.where(linked[None], jnp.exp(jnp.where(linked[None], spread, 0.0)) * scores[None], 0.0).astype(jnp.bfloat16)
    local = jnp.einsum('hst,thp->shp', weight.astype(jnp.float32), upstream.astype(jnp.float32))
    tail = jnp.where((counts == counts[-1])[:, None], jnp.exp(running[-1][None, :] - running), 0.0)
    far = jnp.einsum('hpn,sn->shp', later.astype(jnp.bfloat16).astype(jnp.float32), writes.astype(jnp.float32))
    total = local + tail[:, :, None] * far + gains[None, :, None] * upstream.astype(jnp.float32)
    keep = jnp.where(counts[-1] == 0, jnp.exp(running[-1]), 0.0)
    opened = jnp.where((counts == 0)[:, None], jnp.exp(running), 0.0)
    scaled_map = (opened[:, :, None] * reads.astype(jnp.float32)[:, None, :]).astype(jnp.bfloat16)
    state = jnp.einsum('thp,thn->hpn', upstream.astype(jnp.float32), scaled_map.astype(jnp.float32))
    return (total.astype(jnp.bfloat16), keep, state)

def section_grad(items):
    upstream, writes, reads, decays, marks, gains, projection = items
    blocks = TOKENS // SPAN
    grads = upstream.reshape(blocks, SPAN, H, P_SIZE)
    write_blocks = writes.reshape(blocks, SPAN, N)
    read_blocks = reads.reshape(blocks, SPAN, N)
    decay_blocks = decays.reshape(blocks, SPAN, H)
    mark_blocks = marks.reshape(blocks, SPAN)

    def one_block(later, item):
        grad_block, write_block, read_block, decay_block, mark_block = item
        total, keep, state = block_grad(grad_block, write_block, read_block, decay_block, mark_block, gains, later)
        return (state + keep[:, None, None] * later, total)
    start = jnp.zeros((H, P_SIZE, N), jnp.float32)
    _, pieces = lax.scan(one_block, start, (grads, write_blocks, read_blocks, decay_blocks, mark_blocks), reverse=True)
    scan_grad = pieces.reshape(TOKENS, H * P_SIZE)
    feature_grad = jnp.dot(scan_grad.astype(jnp.float32), projection.astype(jnp.float32).T)
    return feature_grad.astype(jnp.bfloat16)

def reference(cotangent, input_map, output_map, log_decay, flight_starts, skip_gain, in_weight):
    grads = lax.map(section_grad, (cotangent, input_map, output_map, log_decay, flight_starts, skip_gain, in_weight))
    return jnp.roll(grads, -1, axis=0)
```

```python
import functools

import jax
import jax.numpy as jnp
from jax import lax
from jax.experimental import pallas as pl
from jax.experimental.pallas import tpu as pltpu
from jax.sharding import PartitionSpec as P

CHUNK = 128
GROUP = 4
EXTRA = 16
BF16 = jnp.bfloat16
F32 = jnp.float32


def cycle_of(n):
    columns = 1
    while (2 * columns) ** 2 <= n:
        columns *= 2
    rows = n // columns
    if columns == 1:
        return list(range(n))
    order = []
    for z in range(rows):
        ys = range(1, columns)
        order += [z * columns + y for y in (ys if z % 2 == 0 else reversed(ys))]
    return order + [z * columns for z in reversed(range(rows))]


def state_kernel(reads_ref, open_ref, cot_ref, keep_ref, out_ref):
    reads = reads_ref[...].astype(F32)
    width = reads.shape[0]
    for j in range(GROUP):
        scaled = (reads * open_ref[0, j : j + 1, :]).astype(BF16)
        state = jnp.dot(
            scaled, cot_ref[:, j * 128 : (j + 1) * 128], preferred_element_type=F32
        )
        out_ref[j, :width, :] = state.astype(BF16)
        keep = jnp.broadcast_to(keep_ref[0, j : j + 1, :], (EXTRA, 128))
        high = keep.astype(BF16)
        low = (keep - high.astype(F32)).astype(BF16)
        top = lax.broadcasted_iota(jnp.int32, (EXTRA, 128), 0) < EXTRA // 2
        out_ref[j, width:, :] = jnp.where(top, high.astype(F32), low.astype(F32)).astype(BF16)


def fold_kernel(size, width, in_ref, out_ref):
    shape = out_ref.shape[1:]
    later = jnp.zeros(shape, F32)
    for at in reversed(range(size)):
        out_ref[at] = later.astype(BF16)
        if at:
            state = in_ref[at, :, :width, :].astype(F32)
            high = in_ref[at, :, width : width + 1, :].astype(F32)
            low = in_ref[at, :, width + EXTRA // 2 : width + EXTRA // 2 + 1, :].astype(F32)
            later = state + (high + low) * later


def scan_kernel(
    chunks, writes_ref, reads_ref, readst_ref, cntc_ref, cntr_ref, cum_ref, cumt_ref, tail_ref,
    open_ref, keep_ref, gain_ref, cot_ref, later_ref, out_ref, score_ref,
):
    @pl.when(pl.program_id(0) == 0)
    def _():
        row = lax.broadcasted_iota(jnp.int32, (CHUNK, CHUNK), 0)
        col = lax.broadcasted_iota(jnp.int32, (CHUNK, CHUNK), 1)
        for c in range(chunks):
            at = slice(c * CHUNK, (c + 1) * CHUNK)
            scores = lax.dot_general(
                writes_ref[at, :], reads_ref[at, :], (((1,), (1,)), ((), ())),
                preferred_element_type=F32,
            )
            linked = (row <= col) & (cntc_ref[at, :] == cntr_ref[:, at])
            score_ref[at, :] = jnp.where(linked, scores, 0.0)

    for j in range(GROUP):
        lane = slice(j * 128, (j + 1) * 128)
        later = later_ref[j].astype(F32)
        gain = gain_ref[0, j : j + 1, :]
        for c in reversed(range(chunks)):
            at = slice(c * CHUNK, (c + 1) * CHUNK)
            cot = cot_ref[at, lane]
            spread = cumt_ref[0, j : j + 1, at] - cum_ref[0, at, j : j + 1]
            weight = (jnp.exp(jnp.minimum(spread, 0.0)) * score_ref[at, :]).astype(BF16)
            reach = (tail_ref[0, at, j : j + 1] * writes_ref[at, :].astype(F32)).astype(BF16)
            total = jnp.dot(
                jnp.concatenate([weight, reach], axis=1),
                jnp.concatenate([cot, later.astype(BF16)], axis=0),
                preferred_element_type=F32,
            )
            out_ref[at, lane] = (total + gain * cot.astype(F32)).astype(BF16)
            if c:
                scaled = (readst_ref[:, at].astype(F32) * open_ref[0, j : j + 1, at]).astype(BF16)
                state = jnp.dot(scaled, cot, preferred_element_type=F32)
                later = state + keep_ref[0, c * GROUP + j : c * GROUP + j + 1, :] * later


def body(n, cotangent, input_map, output_map, log_decay, flight_starts, skip_gain, in_weight):
    cot = cotangent[0]
    writes, reads = input_map[0], output_map[0]
    heads = skip_gain.shape[1]
    width = writes.shape[1]
    tokens = cot.shape[0]
    size = cot.shape[1] // heads
    chunks = tokens // CHUNK
    groups = heads // GROUP
    mine = lax.axis_index("seq")

    cum = jnp.cumsum(log_decay[0].reshape(chunks, CHUNK, heads), axis=1)
    cnt = jnp.cumsum(flight_starts[0].reshape(chunks, CHUNK), axis=1)
    last, ends = cum[:, -1, :], cnt[:, -1]
    clear = (ends == 0)[:, None]
    keep = jnp.where(clear, jnp.exp(last), 0.0)
    tail = jnp.where((cnt == ends[:, None])[..., None], jnp.exp(last[:, None, :] - cum), 0.0)
    opened = jnp.where((cnt == 0)[..., None], jnp.exp(cum), 0.0)
    before = jnp.cumsum(last, axis=0) - last
    blocked = jnp.cumsum(ends) - ends
    whole = jnp.where(
        ((cnt == 0) & (blocked == 0)[:, None])[..., None], jnp.exp(cum + before[:, None, :]), 0.0
    )
    device_keep = jnp.where(jnp.sum(ends) == 0, jnp.exp(jnp.sum(last, axis=0)), 0.0)

    def rows_of(x):
        return x.reshape(tokens, groups, GROUP).transpose(1, 2, 0)

    def columns_of(x):
        return x.reshape(tokens, groups, GROUP).transpose(1, 0, 2)

    def wide(x):
        return jnp.broadcast_to(x[..., None], x.shape + (128,))

    reads_t = reads.T
    step3 = lambda g: (g, 0, 0)
    whole2 = lambda g: (0, 0)
    states = pl.pallas_call(
        state_kernel,
        grid=(groups,),
        in_specs=[
            pl.BlockSpec((width, tokens), whole2),
            pl.BlockSpec((1, GROUP, tokens), step3),
            pl.BlockSpec((tokens, GROUP * size), lambda g: (0, g)),
            pl.BlockSpec((1, GROUP, 128), step3),
        ],
        out_specs=pl.BlockSpec((GROUP, width + EXTRA, size), step3),
        out_shape=jax.ShapeDtypeStruct((heads, width + EXTRA, size), BF16),
        cost_estimate=pl.CostEstimate(
            flops=2 * tokens * width * heads * size,
            bytes_accessed=2 * tokens * heads * size,
            transcendentals=0,
        ),
        name="states",
    )(reads_t, rows_of(whole), cot, wide(device_keep.reshape(groups, GROUP)))

    held = lax.all_to_all(states, "seq", 0, 0, tiled=True)
    part = heads // n
    held = held.reshape(n, part, width + EXTRA, size)
    entering = pl.pallas_call(
        functools.partial(fold_kernel, n, width),
        out_shape=jax.ShapeDtypeStruct((n, part, width, size), BF16),
        cost_estimate=pl.CostEstimate(
            flops=2 * heads * width * size, bytes_accessed=4 * heads * width * size,
            transcendentals=0,
        ),
        name="fold",
    )(held)
    later = lax.all_to_all(entering.reshape(heads, width, size), "seq", 0, 0, tiled=True)

    scan_grad = pl.pallas_call(
        functools.partial(scan_kernel, chunks),
        grid=(groups,),
        in_specs=[
            pl.BlockSpec((tokens, width), whole2),
            pl.BlockSpec((tokens, width), whole2),
            pl.BlockSpec((width, tokens), whole2),
            pl.BlockSpec((tokens, 1), whole2),
            pl.BlockSpec((1, tokens), whole2),
            pl.BlockSpec((1, tokens, GROUP), step3),
            pl.BlockSpec((1, GROUP, tokens), step3),
            pl.BlockSpec((1, tokens, GROUP), step3),
            pl.BlockSpec((1, GROUP, tokens), step3),
            pl.BlockSpec((1, chunks * GROUP, 128), step3),
            pl.BlockSpec((1, GROUP, 128), step3),
            pl.BlockSpec((tokens, GROUP * size), lambda g: (0, g)),
            pl.BlockSpec((GROUP, width, size), step3),
        ],
        out_specs=pl.BlockSpec((tokens, GROUP * size), lambda g: (0, g)),
        out_shape=jax.ShapeDtypeStruct((tokens, heads * size), BF16),
        scratch_shapes=[pltpu.VMEM((tokens, CHUNK), F32)],
        cost_estimate=pl.CostEstimate(
            flops=6 * tokens * CHUNK * heads * size,
            bytes_accessed=4 * tokens * heads * size,
            transcendentals=tokens * CHUNK * heads,
        ),
        name="scan",
    )(
        writes, reads, reads_t, cnt.reshape(tokens, 1), cnt.reshape(1, tokens),
        columns_of(cum.reshape(tokens, heads)), rows_of(cum), columns_of(tail),
        rows_of(opened),
        wide(keep.reshape(chunks, groups, GROUP).transpose(1, 0, 2).reshape(groups, -1)),
        wide(skip_gain[0].reshape(groups, GROUP)), cot, later,
    )

    order = cycle_of(n)
    place = [order.index(s) for s in range(n)]
    forth = [(order[i], order[(i + 1) % n]) for i in range(n)]
    back = [(b, a) for a, b in forth]
    pipes = lax.axis_size("pipe")
    route = [(i, (i - 1) % pipes) for i in range(pipes)]
    weight = in_weight[0]
    rows = weight.shape[0]
    half = rows // 2
    table = jnp.array(
        [[order[(place[s] - k) % n] for k in range(n)] for s in range(n)], jnp.int32
    )[mine]
    result = jnp.zeros((tokens, n * rows), BF16)

    def finish(result, block, source, offset):
        piece = lax.dot_general(
            scan_grad, block, (((1,), (1,)), ((), ())), preferred_element_type=F32
        ).astype(BF16)
        piece = lax.ppermute(piece, "pipe", route)
        return lax.dynamic_update_slice(result, piece, (0, source * rows + offset))

    result = finish(result, weight, mine, 0)
    streams = []
    for h in range(2):
        for way in (1, -1):
            steps = n // 2 - (0 if (h == 0) == (way == 1) else 1)
            streams.append([weight[h * half : (h + 1) * half], h * half, way, steps])
    for k in range(1, n // 2 + 1):
        for stream in streams:
            block, offset, way, steps = stream
            if k <= steps:
                block = lax.ppermute(block, "seq", forth if way == 1 else back)
                stream[0] = block
                result = finish(result, block, table[(way * k) % n], offset)
    return result[None]


def solution(mesh):
    n = mesh.shape["seq"]
    placed = (
        P("pipe", "seq", None),
        P("pipe", "seq", None),
        P("pipe", "seq", None),
        P("pipe", "seq", None),
        P("pipe", "seq"),
        P("pipe", None),
        P("pipe", "seq", None),
    )
    return jax.shard_map(
        functools.partial(body, n),
        mesh=mesh,
        in_specs=placed,
        out_specs=P("pipe", "seq", None),
        check_vma=False,
    )
```

```python
import functools

import jax
import jax.numpy as jnp
from jax import lax
from jax.experimental import pallas as pl
from jax.experimental.pallas import tpu as pltpu
from jax.sharding import PartitionSpec as P

CHUNK = 128
GROUP = 4
EXTRA = 16
BF16 = jnp.bfloat16
F32 = jnp.float32
COST = pl.CostEstimate(flops=0, bytes_accessed=0, transcendentals=0)


def near_kernel(
    chunks, maps_ref, readst_ref, cntc_ref, cntr_ref, cum_ref, cumt_ref, tail_ref,
    open_ref, keep_ref, whole_ref, gain_ref, cot_ref, out_ref, state_ref, score_ref,
):
    @pl.when(pl.program_id(0) == 0)
    def _():
        row = lax.broadcasted_iota(jnp.int32, (CHUNK, CHUNK), 0)
        col = lax.broadcasted_iota(jnp.int32, (CHUNK, CHUNK), 1)
        for c in range(chunks):
            at = slice(c * CHUNK, (c + 1) * CHUNK)
            scores = lax.dot_general(
                maps_ref[0, at, :], maps_ref[1, at, :], (((1,), (1,)), ((), ())),
                preferred_element_type=F32,
            )
            linked = (row <= col) & (cntc_ref[at, :] == cntr_ref[:, at])
            score_ref[at, :] = jnp.where(linked, scores, 0.0)

    width = readst_ref.shape[0]
    for j in range(GROUP):
        lane = slice(j * 128, (j + 1) * 128)
        gain = gain_ref[0, j : j + 1, :]
        later = None
        for c in reversed(range(chunks)):
            at = slice(c * CHUNK, (c + 1) * CHUNK)
            cot = cot_ref[at, lane]
            spread = cumt_ref[0, j : j + 1, at] - cum_ref[0, at, j : j + 1]
            weight = (jnp.exp(jnp.minimum(spread, 0.0)) * score_ref[at, :]).astype(BF16)
            if later is None:
                total = jnp.dot(weight, cot, preferred_element_type=F32)
            else:
                reach = (tail_ref[0, at, j : j + 1] * maps_ref[0, at, :].astype(F32)).astype(BF16)
                total = jnp.dot(
                    jnp.concatenate([weight, reach], axis=1),
                    jnp.concatenate([cot, later.astype(BF16)], axis=0),
                    preferred_element_type=F32,
                )
            out_ref[at, lane] = (total + gain * cot.astype(F32)).astype(BF16)
            scaled = (readst_ref[:, at].astype(F32) * open_ref[0, j : j + 1, at]).astype(BF16)
            state = jnp.dot(scaled, cot, preferred_element_type=F32)
            if later is not None:
                state = state + keep_ref[0, c * GROUP + j : c * GROUP + j + 1, :] * later
            later = state
        state_ref[j, :width, :] = later.astype(BF16)
        keep = jnp.broadcast_to(whole_ref[0, j : j + 1, :], (EXTRA, 128))
        high = keep.astype(BF16)
        low = (keep - high.astype(F32)).astype(BF16)
        top = lax.broadcasted_iota(jnp.int32, (EXTRA, 128), 0) < EXTRA // 2
        state_ref[j, width:, :] = jnp.where(top, high.astype(F32), low.astype(F32)).astype(BF16)


def far_kernel(*refs):
    near, writes, reach, later, out_ref = refs[0:2], refs[2:4], refs[4:6], refs[6:8], refs[8]
    tokens = near[0].shape[0]
    for side in range(2):
        for j in range(GROUP):
            lane = slice(j * 128, (j + 1) * 128)
            far = jnp.dot(writes[side][0], later[side][j], preferred_element_type=F32)
            total = near[side][:, lane].astype(F32) + reach[side][0, :, j : j + 1] * far
            out_ref[side * tokens : (side + 1) * tokens, lane] = total.astype(BF16)


def gate(x, *after):
    return lax.optimization_barrier((x,) + after)[0]


def step3(g):
    return (g, 0, 0)


def whole2(g):
    return (0, 0)


def columns2(g):
    return (0, g)


def prep_kernel(
    chunks, heads, ext_ref, maps_ref, cumc_ref, tailc_ref, reachc_ref, cumr_ref, openr_ref,
    keep_ref, whole_ref, cntc_ref, cntr_ref, readst_ref,
):
    rows = ext_ref.shape[0]
    groups = heads // GROUP
    col = lax.broadcasted_iota(jnp.int32, (rows, CHUNK), 1)
    after = jnp.zeros((rows, 1), F32)
    for c in reversed(range(chunks)):
        at = slice(c * CHUNK, (c + 1) * CHUNK)
        cum = ext_ref[:, at]
        shift = 1
        while shift < CHUNK:
            cum = cum + jnp.where(col >= shift, pltpu.roll(cum, shift, axis=1), 0.0)
            shift *= 2
        last = cum[:, CHUNK - 1 :]
        cnt, end = cum[heads : heads + 1], last[heads : heads + 1]
        linked = jnp.where(cnt == end, 1.0, 0.0)
        tail = jnp.exp(jnp.minimum(last - cum, 0.0)) * linked
        later = jnp.where(after[heads : heads + 1] == 0.0, jnp.exp(after), 0.0)
        reach = tail * later
        opened = jnp.exp(cum) * jnp.where(cnt == 0.0, 1.0, 0.0)
        keep = jnp.where(end == 0.0, jnp.exp(last), 0.0)
        after = after + last
        cntr_ref[:, at] = cnt
        columns = cum.T
        cntc_ref[at, :] = columns[:, heads : heads + 1]
        tails, reaches = tail.T, reach.T
        for g in range(groups):
            lane = slice(g * GROUP, (g + 1) * GROUP)
            cumr_ref[g, :, at] = cum[lane]
            openr_ref[g, :, at] = opened[lane]
            keep_ref[g, c * GROUP : (c + 1) * GROUP, :] = jnp.broadcast_to(
                keep[lane], (GROUP, 128)
            )
            cumc_ref[g, at, :] = columns[:, lane]
            tailc_ref[g, at, :] = tails[:, lane]
            reachc_ref[g, at, :] = reaches[:, lane]
    whole = jnp.where(after[heads : heads + 1] == 0.0, jnp.exp(after), 0.0)
    for g in range(groups):
        whole_ref[g] = jnp.broadcast_to(whole[g * GROUP : (g + 1) * GROUP], (GROUP, 128))
    readst_ref[...] = maps_ref[1].astype(F32).T.astype(BF16)


def near_part(cot, maps, ext, gains):
    heads = gains.shape[0]
    tokens, width = maps.shape[1:]
    size = cot.shape[1] // heads
    chunks = tokens // CHUNK
    groups = heads // GROUP

    def like(*shape):
        return jax.ShapeDtypeStruct(shape, F32)

    def wide(x):
        return jnp.broadcast_to(x[..., None], x.shape + (128,))

    cumc, tailc, reachc, cumr, openr, keep, whole, cntc, cntr, reads_t = pl.pallas_call(
        functools.partial(prep_kernel, chunks, heads),
        out_shape=[like(groups, tokens, GROUP)] * 3
        + [like(groups, GROUP, tokens)] * 2
        + [like(groups, chunks * GROUP, 128), like(groups, GROUP, 128), like(tokens, 1)]
        + [like(1, tokens), jax.ShapeDtypeStruct((width, tokens), BF16)],
        cost_estimate=COST,
        name="prep",
    )(ext, maps)
    near, state = pl.pallas_call(
        functools.partial(near_kernel, chunks),
        grid=(groups,),
        in_specs=[
            pl.BlockSpec((2, tokens, width), lambda g: (0, 0, 0)),
            pl.BlockSpec((width, tokens), whole2),
            pl.BlockSpec((tokens, 1), whole2),
            pl.BlockSpec((1, tokens), whole2),
            pl.BlockSpec((1, tokens, GROUP), step3),
            pl.BlockSpec((1, GROUP, tokens), step3),
            pl.BlockSpec((1, tokens, GROUP), step3),
            pl.BlockSpec((1, GROUP, tokens), step3),
            pl.BlockSpec((1, chunks * GROUP, 128), step3),
            pl.BlockSpec((1, GROUP, 128), step3),
            pl.BlockSpec((1, GROUP, 128), step3),
            pl.BlockSpec((tokens, GROUP * size), columns2),
        ],
        out_specs=[
            pl.BlockSpec((tokens, GROUP * size), columns2),
            pl.BlockSpec((GROUP, width + EXTRA, size), step3),
        ],
        out_shape=[
            jax.ShapeDtypeStruct((tokens, heads * size), BF16),
            jax.ShapeDtypeStruct((heads, width + EXTRA, size), BF16),
        ],
        scratch_shapes=[pltpu.VMEM((tokens, CHUNK), F32)],
        cost_estimate=COST,
        name="near",
    )(
        maps, reads_t, cntc, cntr, cumc, cumr, tailc, openr, keep, whole,
        wide(gains.reshape(groups, GROUP)), cot,
    )
    return near, state, reachc


def arrivals(m):
    plan = []
    for q in range(m):
        order = [(0, 0)]
        for k in range(1, m):
            order += [(1, k)] * (q >= k) + [(-1, k)] * (q + k < m)
        plan.append(order)
    return plan


def product_kernel(which, tiles, slab_ref, x_ref, *refs):
    blocks, (own_ref, other_ref, held, sem) = refs[:-4], refs[-4:]
    step = pl.program_id(0)

    @pl.when(step == 0)
    def _():
        for b, block in enumerate(blocks):
            chosen = functools.reduce(
                jnp.logical_or, [slab_ref[0] == q for q, w in enumerate(which) if w == b]
            )

            @pl.when(chosen)
            def _():
                copy = pltpu.make_async_copy(block, held, sem)
                copy.start()
                copy.wait()

    piece = lax.dot_general(
        x_ref[...], held[...], (((1,), (1,)), ((), ())), preferred_element_type=F32
    ).astype(BF16)

    @pl.when(step < tiles)
    def _():
        own_ref[...] = piece

    @pl.when(step >= tiles)
    def _():
        other_ref[...] = piece


def product(x, picked, slab, tokens):
    distinct, which = [], []
    for p in picked:
        at = [i for i, d in enumerate(distinct) if d is p]
        which.append(at[0] if at else len(distinct))
        if not at:
            distinct.append(p)
    rows, depth = picked[0].shape
    tile = 256
    tiles = tokens // tile
    return pl.pallas_call(
        functools.partial(product_kernel, which, tiles),
        grid_spec=pltpu.PrefetchScalarGridSpec(
            num_scalar_prefetch=1,
            grid=(2 * tiles,),
            in_specs=[pl.BlockSpec((tile, depth), lambda i, slab: (i, 0))]
            + [pl.BlockSpec(memory_space=pl.ANY)] * len(distinct),
            out_specs=[
                pl.BlockSpec((tile, rows), lambda i, slab: (jnp.minimum(i, tiles - 1), 0)),
                pl.BlockSpec((tile, rows), lambda i, slab: (jnp.maximum(i - tiles, 0), 0)),
            ],
            scratch_shapes=[pltpu.VMEM((rows, depth), BF16), pltpu.SemaphoreType.DMA],
        ),
        out_shape=[jax.ShapeDtypeStruct((tokens, rows), BF16)] * 2,
        cost_estimate=COST,
        name="product",
    )(slab.reshape(1), x, *distinct)


def parts_of(packed, width):
    state = packed[:, :width, :].astype(F32)
    high = packed[:, width : width + 1, :].astype(F32)
    low = packed[:, width + EXTRA // 2 : width + EXTRA // 2 + 1, :].astype(F32)
    return state, high + low


def body(n, pipes, cotangent, input_map, output_map, log_decay, flight_starts, skip_gain, in_weight):
    cot = cotangent[0]
    gains = skip_gain[0]
    heads = gains.shape[0]
    tokens, width = input_map.shape[1:]
    maps = jnp.concatenate([input_map, output_map], axis=0)
    starts = jnp.broadcast_to(flight_starts.astype(F32), (8, tokens))
    ext = jnp.concatenate([log_decay[0].T, starts], axis=0)
    size = cot.shape[1] // heads
    groups = heads // GROUP
    m = n // 2
    mine = lax.axis_index("seq")
    slab, side = mine // 2, mine % 2
    first = side == 0

    pair = [(s, s ^ 1) for s in range(n)]

    def swap(x):
        return lax.ppermute(x, "seq", pair)

    ext_b, maps_b = swap(ext), swap(maps)
    cot_b = swap(cot)

    weight = in_weight[0]
    blocks = {(0, 0): weight}
    for k in range(1, m):
        blocks[1, k] = lax.ppermute(
            blocks.get((1, k - 1), weight), "seq",
            [(s, s + 2) for s in range(2 * (k - 1), n - 2)],
        )
        blocks[-1, k] = lax.ppermute(
            blocks.get((-1, k - 1), weight), "seq",
            [(s, s - 2) for s in range(2, n - 2 * (k - 1))],
        )

    near_a, state_a, reach_a = near_part(gate(cot, ext_b, maps_b), maps, ext, gains)
    half = heads // 2
    got = swap(lax.dynamic_slice_in_dim(state_a, (1 - side) * half, half, 0))
    kept = lax.dynamic_slice_in_dim(state_a, side * half, half, 0)
    state_0, keep_0 = parts_of(jnp.where(first, kept, got), width)
    state_1, keep_1 = parts_of(jnp.where(first, got, kept), width)
    slab_state, slab_keep = state_0 + keep_0 * state_1, keep_0 * keep_1
    later = jnp.zeros((half, width, size), BF16)
    for at in reversed(range(1, m)):
        leaving = (slab_state + slab_keep * later.astype(F32)).astype(BF16)
        if at == m - 1:
            leaving = gate(leaving, blocks[1, 1], blocks[-1, 1])
        later = later + lax.ppermute(
            leaving, "seq", [(2 * at + y, 2 * at - 2 + y) for y in range(2)]
        )
    other = swap(later)
    last = jnp.where(first, jnp.stack([later, other]), jnp.stack([other, later]))
    last = last.reshape(heads, width, size)

    near_b, state_b, reach_b = near_part(cot_b, maps_b, ext_b, gains)
    state_1, keep_1 = parts_of(jnp.where(first, state_b, state_a), width)
    early = (state_1 + keep_1 * last.astype(F32)).astype(BF16)
    later_a = jnp.where(first, early, last)
    later_b = jnp.where(first, last, early)

    block2 = pl.BlockSpec((tokens, GROUP * size), columns2)
    scan_grad = pl.pallas_call(
        far_kernel,
        grid=(groups,),
        in_specs=[block2] * 2
        + [pl.BlockSpec((1, tokens, width), lambda g: (0, 0, 0))] * 2
        + [pl.BlockSpec((1, tokens, GROUP), step3)] * 2
        + [pl.BlockSpec((GROUP, width, size), step3)] * 2,
        out_specs=pl.BlockSpec((2 * tokens, GROUP * size), columns2),
        out_shape=jax.ShapeDtypeStruct((2 * tokens, heads * size), BF16),
        cost_estimate=COST,
        name="far",
    )(near_a, near_b, maps, maps_b, reach_a, reach_b, later_a, later_b)

    rows = weight.shape[0]
    result = jnp.zeros((tokens, n * rows), BF16)
    plan = arrivals(m)
    for slot in range(m):
        picks = [plan[q][slot] for q in range(m)]
        got = product(scan_grad, [blocks[p] for p in picks], slab, tokens)
        source = jnp.array([q - way * k for q, (way, k) in enumerate(picks)], jnp.int32)[slab]
        for flip in range(2):
            route = [
                (s * pipes + p, (s ^ flip) * pipes + (p - 1) % pipes)
                for s in range(n) for p in range(pipes)
            ]
            piece = lax.ppermute(got[flip], ("seq", "pipe"), route)
            column = (2 * source + (side ^ flip)) * rows
            result = lax.dynamic_update_slice(result, piece, (0, column))
    return result[None]


def solution(mesh):
    n, pipes = mesh.shape["seq"], mesh.shape["pipe"]
    placed = (
        P("pipe", "seq", None),
        P("pipe", "seq", None),
        P("pipe", "seq", None),
        P("pipe", "seq", None),
        P("pipe", "seq"),
        P("pipe", None),
        P("pipe", "seq", None),
    )
    return jax.shard_map(
        functools.partial(body, n, pipes),
        mesh=mesh,
        in_specs=placed,
        out_specs=P("pipe", "seq", None),
        check_vma=False,
    )
```

```python
import functools

import jax
import jax.numpy as jnp
from jax import lax
from jax.experimental import pallas as pl
from jax.experimental.pallas import tpu as pltpu
from jax.sharding import PartitionSpec as P

CHUNK = 128
GROUP = 4
EXTRA = 16
SLOTS = 3
TILE = 256
BF16 = jnp.bfloat16
F32 = jnp.float32
COST = pl.CostEstimate(flops=0, bytes_accessed=0, transcendentals=0)


def turned(cols_ref, first):
    lanes = cols_ref.shape[1]
    return pltpu.roll(
        cols_ref[...], lax.rem(2 * lanes - first - GROUP * pl.program_id(0), lanes), axis=1
    )


def prep_kernel(
    chunks, heads, decay_ref, starts_ref, reads_ref,
    cols_ref, cumr_ref, openr_ref, keep_ref, whole_ref, cntr_ref, readst_ref,
):
    groups = heads // GROUP
    rows = heads + 8
    col = lax.broadcasted_iota(jnp.int32, (rows, CHUNK), 1)
    after = jnp.zeros((rows, 1), F32)
    for c in reversed(range(chunks)):
        at = slice(c * CHUNK, (c + 1) * CHUNK)
        decay = jnp.concatenate(
            [decay_ref[at, :], jnp.zeros((CHUNK, CHUNK - heads), F32)], axis=1
        ).T[:heads]
        starts = jnp.broadcast_to(starts_ref[:, at].astype(F32), (8, CHUNK))
        cum = jnp.concatenate([decay, starts], axis=0)
        shift = 1
        while shift < CHUNK:
            cum = cum + jnp.where(col >= shift, pltpu.roll(cum, shift, axis=1), 0.0)
            shift *= 2
        last = cum[:, CHUNK - 1 :]
        cnt, end = cum[heads : heads + 1], last[heads : heads + 1]
        linked = jnp.where(cnt == end, 1.0, 0.0)
        tail = jnp.exp(jnp.minimum(last - cum, 0.0)) * linked
        later = jnp.where(after[heads : heads + 1] == 0.0, jnp.exp(after), 0.0)
        reach = tail * later
        opened = jnp.exp(cum) * jnp.where(cnt == 0.0, 1.0, 0.0)
        keep = jnp.where(end == 0.0, jnp.exp(last), 0.0)
        after = after + last
        cntr_ref[:, at] = cnt
        stack = [cum, tail[:heads], reach[:heads]]
        stack.append(jnp.zeros((CHUNK - 3 * heads - 8, CHUNK), F32))
        cols_ref[at, :] = jnp.concatenate(stack, axis=0).T
        for g in range(groups):
            lane = slice(g * GROUP, (g + 1) * GROUP)
            cumr_ref[g, :, at] = cum[lane]
            openr_ref[g, :, at] = opened[lane]
            keep_ref[g, c * GROUP : (c + 1) * GROUP, :] = jnp.broadcast_to(
                keep[lane], (GROUP, 128)
            )
    whole = jnp.where(after[heads : heads + 1] == 0.0, jnp.exp(after), 0.0)
    for g in range(groups):
        whole_ref[g] = jnp.broadcast_to(whole[g * GROUP : (g + 1) * GROUP], (GROUP, 128))
    readst_ref[...] = reads_ref[...].astype(F32).T.astype(BF16)


def near_kernel(
    chunks, heads, pieces, gain_ref, writes_ref, reads_ref, readst_ref, cntr_ref, cols_ref,
    cumr_ref, openr_ref, keep_ref, whole_ref, *refs,
):
    cot_refs, (out_ref, state_ref, score_ref) = refs[: len(pieces)], refs[len(pieces) :]
    group = pl.program_id(0)

    @pl.when(group == 0)
    def _():
        row = lax.broadcasted_iota(jnp.int32, (CHUNK, CHUNK), 0)
        col = lax.broadcasted_iota(jnp.int32, (CHUNK, CHUNK), 1)
        for c in range(chunks):
            at = slice(c * CHUNK, (c + 1) * CHUNK)
            scores = lax.dot_general(
                writes_ref[at, :], reads_ref[at, :], (((1,), (1,)), ((), ())),
                preferred_element_type=F32,
            )
            linked = (row <= col) & (cols_ref[at, heads : heads + 1] == cntr_ref[:, at])
            score_ref[at, :] = jnp.where(linked, scores, 0.0)

    cols = turned(cols_ref, 0)
    where = []
    for p, length in enumerate(pieces):
        where += [(p, i) for i in range(length // CHUNK)]
    width = readst_ref.shape[0]
    for j in range(GROUP):
        lane = slice(j * 128, (j + 1) * 128)
        gain = gain_ref[0, group * GROUP + j]
        later = None
        for c in reversed(range(chunks)):
            at = slice(c * CHUNK, (c + 1) * CHUNK)
            piece, inner = where[c]
            cot = cot_refs[piece][inner * CHUNK : (inner + 1) * CHUNK, lane]
            spread = cumr_ref[0, j : j + 1, at] - cols[at, j : j + 1]
            weight = (jnp.exp(jnp.minimum(spread, 0.0)) * score_ref[at, :]).astype(BF16)
            if later is None:
                total = jnp.dot(weight, cot, preferred_element_type=F32)
            else:
                tail = cols[at, heads + 8 + j : heads + 9 + j]
                reach = (tail * writes_ref[at, :].astype(F32)).astype(BF16)
                total = jnp.dot(
                    jnp.concatenate([weight, reach], axis=1),
                    jnp.concatenate([cot, later.astype(BF16)], axis=0),
                    preferred_element_type=F32,
                )
            out_ref[at, lane] = (total + gain * cot.astype(F32)).astype(BF16)
            scaled = (readst_ref[:, at].astype(F32) * openr_ref[0, j : j + 1, at]).astype(BF16)
            state = jnp.dot(scaled, cot, preferred_element_type=F32)
            if later is not None:
                state = state + keep_ref[0, c * GROUP + j : c * GROUP + j + 1, :] * later
            later = state
        state_ref[j, :width, :] = later.astype(BF16)
        keep = jnp.broadcast_to(whole_ref[0, j : j + 1, :], (EXTRA, 128))
        high = keep.astype(BF16)
        low = (keep - high.astype(F32)).astype(BF16)
        top = lax.broadcasted_iota(jnp.int32, (EXTRA, 128), 0) < EXTRA // 2
        state_ref[j, width:, :] = jnp.where(top, high.astype(F32), low.astype(F32)).astype(BF16)


def fetch(slab_ref, which, blocks, held, sem):
    for b, block in enumerate(blocks):
        chosen = [slab_ref[0] == q for q, w in enumerate(which) if w == b]
        if chosen:

            @pl.when(functools.reduce(jnp.logical_or, chosen))
            def _():
                pltpu.make_async_copy(block, held, sem).start()


def main_kernel(whiches, heads, slab_ref, *refs):
    near, writes, cols, later, refs = refs[0:2], refs[2:4], refs[4:6], refs[6:8], refs[8:]
    weight_ref, refs = refs[0], refs[1:]
    blocks, (x_ref, own_ref, other_ref, acc_ref, held, sems) = refs[:-6], refs[-6:]
    tokens, step_width = near[0].shape
    rows = weight_ref.shape[0]
    step, steps = pl.program_id(0), pl.num_programs(0)

    @pl.when(step == 0)
    def _():
        acc_ref[...] = jnp.zeros_like(acc_ref)
        for i, which in enumerate(whiches):
            fetch(slab_ref, which, blocks, held.at[i], sems.at[i])

    for side in range(2):
        reach = turned(cols[side], 2 * heads + 8)
        for j in range(GROUP):
            lane = slice(j * 128, (j + 1) * 128)
            far = jnp.dot(writes[side][...], later[side][j], preferred_element_type=F32)
            total = near[side][:, lane].astype(F32) + reach[:, j : j + 1] * far
            x_ref[side * tokens : (side + 1) * tokens, lane] = total.astype(BF16)

    @pl.when(step == 0)
    def _():
        for i in range(len(whiches)):
            pltpu.make_async_copy(blocks[0], held.at[i], sems.at[i]).wait()

    depth = pl.ds(pl.multiple_of(step * step_width, step_width), step_width)
    for i in range(len(whiches) + 1):
        block = weight_ref[...] if i == 0 else held[i - 1, :, depth]
        acc_ref[:, i * rows : (i + 1) * rows] += lax.dot_general(
            x_ref[...], block, (((1,), (1,)), ((), ())), preferred_element_type=F32
        )

    @pl.when(step == steps - 1)
    def _():
        own_ref[...] = acc_ref[:tokens].astype(BF16)
        other_ref[...] = acc_ref[tokens:].astype(BF16)


def product_kernel(which, slab_ref, x_ref, *refs):
    blocks, (own_ref, other_ref, held, x_held, sem, x_sems) = refs[:-6], refs[-6:]
    fetch(slab_ref, which, blocks, held, sem)
    tokens = own_ref.shape[0]
    tiles = [
        pltpu.make_async_copy(
            x_ref.at[i * TILE : (i + 1) * TILE], x_held.at[i * TILE : (i + 1) * TILE], x_sems.at[i]
        )
        for i in range(2 * tokens // TILE)
    ]
    for tile in tiles:
        tile.start()
    pltpu.make_async_copy(blocks[0], held, sem).wait()
    for i, tile in enumerate(tiles):
        tile.wait()
        out_ref = own_ref if i * TILE < tokens else other_ref
        at = (i * TILE) % tokens
        out_ref[at : at + TILE, :] = lax.dot_general(
            x_held[i * TILE : (i + 1) * TILE, :], held[...],
            (((1,), (1,)), ((), ())), preferred_element_type=F32,
        ).astype(BF16)


def gate(x, *after):
    return lax.optimization_barrier((x,) + after)[0]


def step3(g, *_):
    return (g, 0, 0)


def whole2(g, *_):
    return (0, 0)


def columns2(g, *_):
    return (0, g)


def prepared(reads, decay, starts):
    tokens, heads = decay.shape
    width = reads.shape[1]
    chunks = tokens // CHUNK
    groups = heads // GROUP

    def like(*shape):
        return jax.ShapeDtypeStruct(shape, F32)

    return pl.pallas_call(
        functools.partial(prep_kernel, chunks, heads),
        out_shape=[like(tokens, CHUNK)]
        + [like(groups, GROUP, tokens)] * 2
        + [like(groups, chunks * GROUP, 128), like(groups, GROUP, 128), like(1, tokens)]
        + [jax.ShapeDtypeStruct((width, tokens), BF16)],
        cost_estimate=COST,
        name="prep",
    )(decay, starts, reads)


def near_part(cots, writes, reads, gains, ready):
    cols, cumr, openr, keep, whole, cntr, reads_t = ready
    heads = gains.shape[1]
    tokens, width = writes.shape
    size = cots[0].shape[1] // heads
    chunks = tokens // CHUNK
    groups = heads // GROUP
    pieces = [c.shape[0] for c in cots]
    return pl.pallas_call(
        functools.partial(near_kernel, chunks, heads, pieces),
        grid=(groups,),
        in_specs=[
            pl.BlockSpec(memory_space=pltpu.SMEM),
            pl.BlockSpec((tokens, width), whole2),
            pl.BlockSpec((tokens, width), whole2),
            pl.BlockSpec((width, tokens), whole2),
            pl.BlockSpec((1, tokens), whole2),
            pl.BlockSpec((tokens, CHUNK), whole2),
            pl.BlockSpec((1, GROUP, tokens), step3),
            pl.BlockSpec((1, GROUP, tokens), step3),
            pl.BlockSpec((1, chunks * GROUP, 128), step3),
            pl.BlockSpec((1, GROUP, 128), step3),
        ]
        + [pl.BlockSpec((length, GROUP * size), columns2) for length in pieces],
        out_specs=[
            pl.BlockSpec((tokens, GROUP * size), columns2),
            pl.BlockSpec((GROUP, width + EXTRA, size), step3),
        ],
        out_shape=[
            jax.ShapeDtypeStruct((tokens, heads * size), BF16),
            jax.ShapeDtypeStruct((heads, width + EXTRA, size), BF16),
        ],
        scratch_shapes=[pltpu.VMEM((tokens, CHUNK), F32)],
        cost_estimate=COST,
        name="near",
    )(gains, writes, reads, reads_t, cntr, cols, cumr, openr, keep, whole, *cots)


def arrivals(m):
    plan = []
    for q in range(m):
        order = [(0, 0)]
        for k in range(1, m):
            order += [(1, k)] * (q >= k) + [(-1, k)] * (q + k < m)
        plan.append(order)
    return plan


def indexed(slots):
    distinct = []
    for picks in slots:
        distinct += [p for p in picks if p not in distinct]
    return distinct, [[distinct.index(p) for p in picks] for picks in slots]


def main_part(near, writes, cols, later, weight, blocks, slots, slab, heads):
    tokens, width = writes[0].shape
    rows, depth = weight.shape
    size = depth // heads
    count = len(slots) + 1
    distinct, whiches = indexed(slots)
    block2 = pl.BlockSpec((tokens, GROUP * size), columns2)
    return pl.pallas_call(
        functools.partial(main_kernel, whiches, heads),
        grid_spec=pltpu.PrefetchScalarGridSpec(
            num_scalar_prefetch=1,
            grid=(heads // GROUP,),
            in_specs=[block2] * 2
            + [pl.BlockSpec((tokens, width), whole2)] * 2
            + [pl.BlockSpec((tokens, CHUNK), whole2)] * 2
            + [pl.BlockSpec((GROUP, width, size), step3)] * 2
            + [pl.BlockSpec((rows, GROUP * size), columns2)]
            + [pl.BlockSpec(memory_space=pl.ANY)] * len(distinct),
            out_specs=[pl.BlockSpec((2 * tokens, GROUP * size), columns2)]
            + [pl.BlockSpec((tokens, count * rows), whole2)] * 2,
            scratch_shapes=[
                pltpu.VMEM((2 * tokens, count * rows), F32),
                pltpu.VMEM((count - 1, rows, depth), BF16),
                pltpu.SemaphoreType.DMA((count - 1,)),
            ],
        ),
        out_shape=[jax.ShapeDtypeStruct((2 * tokens, depth), BF16)]
        + [jax.ShapeDtypeStruct((tokens, count * rows), BF16)] * 2,
        cost_estimate=COST,
        name="main",
    )(slab.reshape(1), *near, *writes, *cols, *later, weight, *[blocks[p] for p in distinct])


def product(x, blocks, picks, slab, tokens):
    distinct, (which,) = indexed([picks])
    rows, depth = blocks[picks[0]].shape
    vmem = pl.BlockSpec(memory_space=pltpu.VMEM)
    return pl.pallas_call(
        functools.partial(product_kernel, which),
        in_specs=[pl.BlockSpec(memory_space=pltpu.SMEM)]
        + [pl.BlockSpec(memory_space=pl.ANY)] * (1 + len(distinct)),
        out_specs=[vmem] * 2,
        scratch_shapes=[
            pltpu.VMEM((rows, depth), BF16),
            pltpu.VMEM(x.shape, BF16),
            pltpu.SemaphoreType.DMA,
            pltpu.SemaphoreType.DMA((x.shape[0] // TILE,)),
        ],
        out_shape=[jax.ShapeDtypeStruct((tokens, rows), BF16)] * 2,
        cost_estimate=COST,
        name="product",
    )(slab.reshape(1), x, *[blocks[p] for p in distinct])


def assemble_kernel(counts, columns_ref, *refs):
    pieces, out_ref = refs[:-1], refs[-1]
    rows = pieces[0].shape[1] // counts[0]
    at = 0
    for piece, count in zip(pieces, counts):
        for i in range(count):
            column = pl.multiple_of(columns_ref[at] * rows, rows)
            out_ref[0, :, pl.ds(column, rows)] = piece[:, i * rows : (i + 1) * rows]
            at += 1


def assembled(pieces, columns, rows):
    counts = [piece.shape[1] // rows for piece in pieces]
    if rows % 128:
        result = jnp.zeros((1, pieces[0].shape[0], sum(counts) * rows), BF16)
        at = 0
        for piece, count in zip(pieces, counts):
            for i in range(count):
                result = lax.dynamic_update_slice(
                    result, piece[None, :, i * rows : (i + 1) * rows], (0, 0, columns[at] * rows)
                )
                at += 1
        return result
    vmem = pl.BlockSpec(memory_space=pltpu.VMEM)
    return pl.pallas_call(
        functools.partial(assemble_kernel, counts),
        in_specs=[pl.BlockSpec(memory_space=pltpu.SMEM)] + [vmem] * len(pieces),
        out_specs=vmem,
        out_shape=jax.ShapeDtypeStruct((1, pieces[0].shape[0], sum(counts) * rows), BF16),
        compiler_params=pltpu.CompilerParams(vmem_limit_bytes=32 << 20),
        cost_estimate=COST,
        name="assemble",
    )(columns, *pieces)


def parts_of(packed, width):
    state = packed[:, :width, :].astype(F32)
    high = packed[:, width : width + 1, :].astype(F32)
    low = packed[:, width + EXTRA // 2 : width + EXTRA // 2 + 1, :].astype(F32)
    return state, high + low


def body(n, pipes, cotangent, input_map, output_map, log_decay, flight_starts, skip_gain, in_weight):
    cot, weight = cotangent[0], in_weight[0]
    writes, reads, decay = input_map[0], output_map[0], log_decay[0]
    tokens, heads = decay.shape
    width = writes.shape[1]
    size = cot.shape[1] // heads
    rows = weight.shape[0]
    m = n // 2
    mine = lax.axis_index("seq")
    slab, side = mine // 2, mine % 2
    first = side == 0

    pair = [(s, s ^ 1) for s in range(n)]

    def swap(x):
        return lax.ppermute(x, "seq", pair)

    def down(k):
        return [(s, s - 2) for s in range(2, n - 2 * (k - 1))]

    blocks = {(0, 0): weight}
    for k in range(1, m):
        blocks[1, k] = lax.ppermute(
            blocks.get((1, k - 1), weight), "seq",
            [(s, s + 2) for s in range(2 * (k - 1), n - 2)],
        )
        if k < m - 1:
            blocks[-1, k] = lax.ppermute(blocks.get((-1, k - 1), weight), "seq", down(k))

    writes_b, reads_b, decay_b, starts_b = [
        swap(x) for x in (writes, reads, decay, flight_starts)
    ]
    small = (writes_b, reads_b, decay_b, starts_b)
    cots_b = [swap(gate(cot[:CHUNK], *small)), swap(cot[CHUNK:])]

    ready_a = prepared(reads, decay, flight_starts)
    near_a, state_a = near_part(
        [gate(cot, *small)], writes, reads, skip_gain, ready_a
    )
    ready_b = prepared(reads_b, decay_b, starts_b)
    half = heads // 2
    leaving = lax.dynamic_slice_in_dim(state_a, (1 - side) * half, half, 0)
    got = swap(gate(leaving, cots_b[0]))
    kept = lax.dynamic_slice_in_dim(state_a, side * half, half, 0)
    state_0, keep_0 = parts_of(jnp.where(first, kept, got), width)
    state_1, keep_1 = parts_of(jnp.where(first, got, kept), width)
    slab_state, slab_keep = state_0 + keep_0 * state_1, keep_0 * keep_1
    later = jnp.zeros((half, width, size), BF16)
    for at in reversed(range(1, m)):
        leaving = (slab_state + slab_keep * later.astype(F32)).astype(BF16)
        if at == m - 1:
            leaving = gate(leaving, blocks[1, 1], blocks[-1, 1], ready_b[0])
        later = later + lax.ppermute(
            leaving, "seq", [(2 * at + y, 2 * at - 2 + y) for y in range(2)]
        )
    blocks[-1, m - 1] = lax.ppermute(gate(blocks[-1, m - 2], later), "seq", down(m - 1))
    other = swap(later)
    cots_b[0] = gate(cots_b[0], later)
    near_b, state_b = near_part(cots_b, writes_b, reads_b, skip_gain, ready_b)
    last = jnp.where(first, jnp.stack([later, other]), jnp.stack([other, later]))
    last = last.reshape(heads, width, size)
    state_1, keep_1 = parts_of(jnp.where(first, state_b, state_a), width)
    early = (state_1 + keep_1 * last.astype(F32)).astype(BF16)
    later_a = jnp.where(first, early, last)
    later_b = jnp.where(first, last, early)

    plan = arrivals(m)
    slots = [[plan[q][slot] for q in range(m)] for slot in range(m)]
    count = min(m - 1, SLOTS)
    x, own, swapped = main_part(
        (near_a, near_b), (writes, writes_b), (ready_a[0], ready_b[0]), (later_a, later_b),
        weight, blocks, slots[1:count], slab, heads,
    )
    todo = [(slots[:count], (own, swapped))]
    for slot in range(count, m):
        todo.append(([slots[slot]], product(x, blocks, slots[slot], slab, tokens)))
    pieces, columns = [], []
    for picked, got in todo:
        table = jnp.array(
            [[2 * (q - way * k) for q, (way, k) in enumerate(picks)] for picks in picked],
            jnp.int32,
        )[:, slab]
        for flip in range(2):
            route = [
                (s * pipes + p, (s ^ flip) * pipes + (p - 1) % pipes)
                for s in range(n) for p in range(pipes)
            ]
            pieces.append(lax.ppermute(got[flip], ("seq", "pipe"), route))
            columns.append(table + (side ^ flip))
    return assembled(pieces, jnp.concatenate(columns), rows)


def solution(mesh):
    n, pipes = mesh.shape["seq"], mesh.shape["pipe"]
    placed = (
        P("pipe", "seq", None),
        P("pipe", "seq", None),
        P("pipe", "seq", None),
        P("pipe", "seq", None),
        P("pipe", "seq"),
        P("pipe", None),
        P("pipe", "seq", None),
    )
    return jax.shard_map(
        functools.partial(body, n, pipes),
        mesh=mesh,
        in_specs=placed,
        out_specs=P("pipe", "seq", None),
        check_vma=False,
    )
```

```python
import functools

import jax
import jax.numpy as jnp
from jax import lax
from jax.experimental import pallas as pl
from jax.experimental.pallas import tpu as pltpu
from jax.sharding import PartitionSpec as P

CHUNK = 128
GROUP = 4
EXTRA = 16
SLOTS = 3
BF16 = jnp.bfloat16
F32 = jnp.float32
COST = pl.CostEstimate(flops=0, bytes_accessed=0, transcendentals=0)


def turned(cols_ref, first):
    lanes = cols_ref.shape[1]
    return pltpu.roll(
        cols_ref[...], lax.rem(2 * lanes - first - GROUP * pl.program_id(0), lanes), axis=1
    )


def prep_kernel(
    chunks, heads, decay_ref, starts_ref, reads_ref,
    cols_ref, cumr_ref, openr_ref, keep_ref, whole_ref, cntr_ref, readst_ref, allr_ref,
):
    groups = heads // GROUP
    rows = heads + 8
    col = lax.broadcasted_iota(jnp.int32, (rows, CHUNK), 1)
    after = jnp.zeros((rows, 1), F32)
    kept = []
    for c in reversed(range(chunks)):
        at = slice(c * CHUNK, (c + 1) * CHUNK)
        decay = jnp.concatenate(
            [decay_ref[at, :], jnp.zeros((CHUNK, CHUNK - heads), F32)], axis=1
        ).T[:heads]
        starts = jnp.broadcast_to(starts_ref[:, at].astype(F32), (8, CHUNK))
        cum = jnp.concatenate([decay, starts], axis=0)
        shift = 1
        while shift < CHUNK:
            cum = cum + jnp.where(col >= shift, pltpu.roll(cum, shift, axis=1), 0.0)
            shift *= 2
        last = cum[:, CHUNK - 1 :]
        cnt, end = cum[heads : heads + 1], last[heads : heads + 1]
        linked = jnp.where(cnt == end, 1.0, 0.0)
        tail = jnp.exp(jnp.minimum(last - cum, 0.0)) * linked
        later = jnp.where(after[heads : heads + 1] == 0.0, jnp.exp(after), 0.0)
        reach = tail * later
        opened = jnp.exp(cum) * jnp.where(cnt == 0.0, 1.0, 0.0)
        keep = jnp.where(end == 0.0, jnp.exp(last), 0.0)
        after = after + last
        kept.append((cum, last))
        cntr_ref[:, at] = cnt
        stack = [cum, tail[:heads], reach[:heads]]
        stack.append(jnp.zeros((CHUNK - 3 * heads - 8, CHUNK), F32))
        cols_ref[at, :] = jnp.concatenate(stack, axis=0).T
        for g in range(groups):
            lane = slice(g * GROUP, (g + 1) * GROUP)
            cumr_ref[g, :, at] = cum[lane]
            openr_ref[g, :, at] = opened[lane]
            keep_ref[g, c * GROUP : (c + 1) * GROUP, :] = jnp.broadcast_to(
                keep[lane], (GROUP, 128)
            )
    whole = jnp.where(after[heads : heads + 1] == 0.0, jnp.exp(after), 0.0)
    for g in range(groups):
        whole_ref[g] = jnp.broadcast_to(whole[g * GROUP : (g + 1) * GROUP], (GROUP, 128))
    before = jnp.zeros((rows, 1), F32)
    for c, (cum, last) in enumerate(reversed(kept)):
        total = cum + before
        opened = jnp.exp(total) * jnp.where(total[heads : heads + 1] == 0.0, 1.0, 0.0)
        before = before + last
        for g in range(groups):
            allr_ref[g, :, c * CHUNK : (c + 1) * CHUNK] = opened[g * GROUP : (g + 1) * GROUP]
    readst_ref[...] = reads_ref[...].astype(F32).T.astype(BF16)


def near_kernel(
    chunks, heads, pieces, gain_ref, writes_ref, reads_ref, readst_ref, cntr_ref, cols_ref,
    cumr_ref, openr_ref, keep_ref, whole_ref, *refs,
):
    cot_refs, out_ref, score_ref = refs[: len(pieces)], refs[len(pieces)], refs[-1]
    state_ref = refs[-2] if len(refs) > len(pieces) + 2 else None
    group = pl.program_id(0)

    @pl.when(group == 0)
    def _():
        row = lax.broadcasted_iota(jnp.int32, (CHUNK, CHUNK), 0)
        col = lax.broadcasted_iota(jnp.int32, (CHUNK, CHUNK), 1)
        for c in range(chunks):
            at = slice(c * CHUNK, (c + 1) * CHUNK)
            scores = lax.dot_general(
                writes_ref[at, :], reads_ref[at, :], (((1,), (1,)), ((), ())),
                preferred_element_type=F32,
            )
            linked = (row <= col) & (cols_ref[at, heads : heads + 1] == cntr_ref[:, at])
            score_ref[at, :] = jnp.where(linked, scores, 0.0)

    cols = turned(cols_ref, 0)
    where = []
    for p, length in enumerate(pieces):
        where += [(p, i) for i in range(length // CHUNK)]
    width = readst_ref.shape[0]
    for j in range(GROUP):
        lane = slice(j * 128, (j + 1) * 128)
        gain = gain_ref[0, group * GROUP + j]
        later = None
        for c in reversed(range(chunks)):
            at = slice(c * CHUNK, (c + 1) * CHUNK)
            piece, inner = where[c]
            cot = cot_refs[piece][inner * CHUNK : (inner + 1) * CHUNK, lane]
            spread = cumr_ref[0, j : j + 1, at] - cols[at, j : j + 1]
            weight = (jnp.exp(jnp.minimum(spread, 0.0)) * score_ref[at, :]).astype(BF16)
            if later is None:
                total = jnp.dot(weight, cot, preferred_element_type=F32)
            else:
                tail = cols[at, heads + 8 + j : heads + 9 + j]
                reach = (tail * writes_ref[at, :].astype(F32)).astype(BF16)
                total = jnp.dot(
                    jnp.concatenate([weight, reach], axis=1),
                    jnp.concatenate([cot, later.astype(BF16)], axis=0),
                    preferred_element_type=F32,
                )
            out_ref[at, lane] = (total + gain * cot.astype(F32)).astype(BF16)
            if c == 0 and state_ref is None:
                continue
            scaled = (readst_ref[:, at].astype(F32) * openr_ref[0, j : j + 1, at]).astype(BF16)
            state = jnp.dot(scaled, cot, preferred_element_type=F32)
            if later is not None:
                state = state + keep_ref[0, c * GROUP + j : c * GROUP + j + 1, :] * later
            later = state
        if state_ref is not None:
            pack(state_ref, j, later, whole_ref[0, j : j + 1, :])


def pack(state_ref, j, state, keep):
    width = state.shape[0]
    state_ref[j, :width, :] = state.astype(BF16)
    keep = jnp.broadcast_to(keep, (EXTRA, 128))
    high = keep.astype(BF16)
    low = (keep - high.astype(F32)).astype(BF16)
    top = lax.broadcasted_iota(jnp.int32, (EXTRA, 128), 0) < EXTRA // 2
    state_ref[j, width:, :] = jnp.where(top, high.astype(F32), low.astype(F32)).astype(BF16)


def states_kernel(readst_ref, allr_ref, whole_ref, cot_ref, state_ref):
    for j in range(GROUP):
        scaled = (readst_ref[...].astype(F32) * allr_ref[0, j : j + 1, :]).astype(BF16)
        state = jnp.dot(scaled, cot_ref[:, j * 128 : (j + 1) * 128], preferred_element_type=F32)
        pack(state_ref, j, state, whole_ref[0, j : j + 1, :])


def fetch(slab_ref, which, blocks, held, sem):
    for b, block in enumerate(blocks):
        chosen = [slab_ref[0] == q for q, w in enumerate(which) if w == b]
        if chosen:

            @pl.when(functools.reduce(jnp.logical_or, chosen))
            def _():
                pltpu.make_async_copy(block, held, sem).start()


def main_kernel(whiches, heads, slab_ref, *refs):
    near, writes, cols, later, refs = refs[0:2], refs[2:4], refs[4:6], refs[6:8], refs[8:]
    weight_ref, refs = refs[0], refs[1:]
    blocks, (x_ref, own_ref, other_ref, acc_ref, held, sems) = refs[:-6], refs[-6:]
    tokens, step_width = near[0].shape
    rows = weight_ref.shape[0]
    step, steps = pl.program_id(0), pl.num_programs(0)

    @pl.when(step == 0)
    def _():
        acc_ref[...] = jnp.zeros_like(acc_ref)
        for i, which in enumerate(whiches):
            fetch(slab_ref, which, blocks, held.at[i], sems.at[i])

    depth = pl.ds(pl.multiple_of(step * step_width, step_width), step_width)
    for side in range(2):
        reach = turned(cols[side], 2 * heads + 8)
        for j in range(GROUP):
            lane = slice(j * 128, (j + 1) * 128)
            at = pl.ds(pl.multiple_of(step * step_width + j * 128, 128), 128)
            far = jnp.dot(writes[side][...], later[side][j], preferred_element_type=F32)
            total = near[side][:, lane].astype(F32) + reach[:, j : j + 1] * far
            x_ref[side * tokens : (side + 1) * tokens, at] = total.astype(BF16)

    @pl.when(step == 0)
    def _():
        for i in range(len(whiches)):
            pltpu.make_async_copy(blocks[0], held.at[i], sems.at[i]).wait()

    for i in range(len(whiches) + 1):
        block = weight_ref[...] if i == 0 else held[i - 1, :, depth]
        acc_ref[:, i * rows : (i + 1) * rows] += lax.dot_general(
            x_ref[:, depth], block, (((1,), (1,)), ((), ())), preferred_element_type=F32
        )

    @pl.when(step == steps - 1)
    def _():
        own_ref[...] = acc_ref[:tokens].astype(BF16)
        other_ref[...] = acc_ref[tokens:].astype(BF16)


def product_kernel(which, slab_ref, x_ref, *refs):
    blocks, (own_ref, other_ref, held, sem) = refs[:-4], refs[-4:]
    fetch(slab_ref, which, blocks, held, sem)
    pltpu.make_async_copy(blocks[0], held, sem).wait()
    tokens = own_ref.shape[0]
    for side, out_ref in enumerate((own_ref, other_ref)):
        out_ref[...] = lax.dot_general(
            x_ref[side * tokens : (side + 1) * tokens, :], held[...],
            (((1,), (1,)), ((), ())), preferred_element_type=F32,
        ).astype(BF16)


def gate(x, *after):
    return lax.optimization_barrier((x,) + after)[0]


def step3(g, *_):
    return (g, 0, 0)


def whole2(g, *_):
    return (0, 0)


def columns2(g, *_):
    return (0, g)


def prepared(reads, decay, starts):
    tokens, heads = decay.shape
    width = reads.shape[1]
    chunks = tokens // CHUNK
    groups = heads // GROUP

    def like(*shape):
        return jax.ShapeDtypeStruct(shape, F32)

    return pl.pallas_call(
        functools.partial(prep_kernel, chunks, heads),
        out_shape=[like(tokens, CHUNK)]
        + [like(groups, GROUP, tokens)] * 2
        + [like(groups, chunks * GROUP, 128), like(groups, GROUP, 128), like(1, tokens)]
        + [jax.ShapeDtypeStruct((width, tokens), BF16), like(groups, GROUP, tokens)],
        cost_estimate=COST,
        name="prep",
    )(decay, starts, reads)


def near_part(cots, writes, reads, gains, ready, states):
    cols, cumr, openr, keep, whole, cntr, reads_t = ready[:7]
    heads = gains.shape[1]
    tokens, width = writes.shape
    size = cots[0].shape[1] // heads
    chunks = tokens // CHUNK
    groups = heads // GROUP
    pieces = [c.shape[0] for c in cots]
    return pl.pallas_call(
        functools.partial(near_kernel, chunks, heads, pieces),
        grid=(groups,),
        in_specs=[
            pl.BlockSpec(memory_space=pltpu.SMEM),
            pl.BlockSpec((tokens, width), whole2),
            pl.BlockSpec((tokens, width), whole2),
            pl.BlockSpec((width, tokens), whole2),
            pl.BlockSpec((1, tokens), whole2),
            pl.BlockSpec((tokens, CHUNK), whole2),
            pl.BlockSpec((1, GROUP, tokens), step3),
            pl.BlockSpec((1, GROUP, tokens), step3),
            pl.BlockSpec((1, chunks * GROUP, 128), step3),
            pl.BlockSpec((1, GROUP, 128), step3),
        ]
        + [pl.BlockSpec((length, GROUP * size), columns2) for length in pieces],
        out_specs=[
            pl.BlockSpec((tokens, GROUP * size), columns2),
            pl.BlockSpec((GROUP, width + EXTRA, size), step3),
        ][: 1 + states],
        out_shape=[
            jax.ShapeDtypeStruct((tokens, heads * size), BF16),
            jax.ShapeDtypeStruct((heads, width + EXTRA, size), BF16),
        ][: 1 + states],
        scratch_shapes=[pltpu.VMEM((tokens, CHUNK), F32)],
        cost_estimate=COST,
        name="near",
    )(gains, writes, reads, reads_t, cntr, cols, cumr, openr, keep, whole, *cots)


def states_part(cot, ready):
    whole, reads_t, allr = ready[4], ready[6], ready[7]
    groups, _, tokens = allr.shape
    width = reads_t.shape[0]
    heads = groups * GROUP
    size = cot.shape[1] // heads
    return pl.pallas_call(
        states_kernel,
        grid=(groups,),
        in_specs=[
            pl.BlockSpec((width, tokens), whole2),
            pl.BlockSpec((1, GROUP, tokens), step3),
            pl.BlockSpec((1, GROUP, 128), step3),
            pl.BlockSpec((tokens, GROUP * size), columns2),
        ],
        out_specs=pl.BlockSpec((GROUP, width + EXTRA, size), step3),
        out_shape=jax.ShapeDtypeStruct((heads, width + EXTRA, size), BF16),
        cost_estimate=COST,
        name="states",
    )(reads_t, allr, whole, cot)


def arrivals(m):
    plan = []
    for q in range(m):
        order = [(0, 0)]
        for k in range(1, m):
            order += [(1, k)] * (q >= k) + [(-1, k)] * (q + k < m)
        plan.append(order)
    return plan


def indexed(slots):
    distinct = []
    for picks in slots:
        distinct += [p for p in picks if p not in distinct]
    return distinct, [[distinct.index(p) for p in picks] for picks in slots]


def main_part(near, writes, cols, later, weight, blocks, slots, slab, heads):
    tokens, width = writes[0].shape
    rows, depth = weight.shape
    size = depth // heads
    count = len(slots) + 1
    distinct, whiches = indexed(slots)
    block2 = pl.BlockSpec((tokens, GROUP * size), columns2)
    return pl.pallas_call(
        functools.partial(main_kernel, whiches, heads),
        grid_spec=pltpu.PrefetchScalarGridSpec(
            num_scalar_prefetch=1,
            grid=(heads // GROUP,),
            in_specs=[block2] * 2
            + [pl.BlockSpec((tokens, width), whole2)] * 2
            + [pl.BlockSpec((tokens, CHUNK), whole2)] * 2
            + [pl.BlockSpec((GROUP, width, size), step3)] * 2
            + [pl.BlockSpec((rows, GROUP * size), columns2)]
            + [pl.BlockSpec(memory_space=pl.ANY)] * len(distinct),
            out_specs=[pl.BlockSpec(memory_space=pltpu.VMEM)]
            + [pl.BlockSpec((tokens, count * rows), whole2)] * 2,
            scratch_shapes=[
                pltpu.VMEM((2 * tokens, count * rows), F32),
                pltpu.VMEM((count - 1, rows, depth), BF16),
                pltpu.SemaphoreType.DMA((count - 1,)),
            ],
        ),
        out_shape=[pltpu.VMEM((2 * tokens, depth), BF16)]
        + [jax.ShapeDtypeStruct((tokens, count * rows), BF16)] * 2,
        compiler_params=pltpu.CompilerParams(vmem_limit_bytes=36 << 20),
        cost_estimate=COST,
        name="main",
    )(slab.reshape(1), *near, *writes, *cols, *later, weight, *[blocks[p] for p in distinct])


def product(x, blocks, picks, slab, tokens):
    distinct, (which,) = indexed([picks])
    rows, depth = blocks[picks[0]].shape
    vmem = pl.BlockSpec(memory_space=pltpu.VMEM)
    return pl.pallas_call(
        functools.partial(product_kernel, which),
        in_specs=[pl.BlockSpec(memory_space=pltpu.SMEM), vmem]
        + [pl.BlockSpec(memory_space=pl.ANY)] * len(distinct),
        out_specs=[vmem] * 2,
        scratch_shapes=[
            pltpu.VMEM((rows, depth), BF16),
            pltpu.SemaphoreType.DMA,
        ],
        out_shape=[jax.ShapeDtypeStruct((tokens, rows), BF16)] * 2,
        compiler_params=pltpu.CompilerParams(vmem_limit_bytes=24 << 20),
        cost_estimate=COST,
        name="product",
    )(slab.reshape(1), x, *[blocks[p] for p in distinct])


def assemble_kernel(counts, columns_ref, *refs):
    pieces, out_ref = refs[:-1], refs[-1]
    rows = pieces[0].shape[1] // counts[0]
    at = 0
    for piece, count in zip(pieces, counts):
        for i in range(count):
            column = pl.multiple_of(columns_ref[at] * rows, rows)
            out_ref[0, :, pl.ds(column, rows)] = piece[:, i * rows : (i + 1) * rows]
            at += 1


def assembled(pieces, columns, rows):
    counts = [piece.shape[1] // rows for piece in pieces]
    if rows % 128:
        result = jnp.zeros((1, pieces[0].shape[0], sum(counts) * rows), BF16)
        at = 0
        for piece, count in zip(pieces, counts):
            for i in range(count):
                result = lax.dynamic_update_slice(
                    result, piece[None, :, i * rows : (i + 1) * rows], (0, 0, columns[at] * rows)
                )
                at += 1
        return result
    vmem = pl.BlockSpec(memory_space=pltpu.VMEM)
    return pl.pallas_call(
        functools.partial(assemble_kernel, counts),
        in_specs=[pl.BlockSpec(memory_space=pltpu.SMEM)] + [vmem] * len(pieces),
        out_specs=vmem,
        out_shape=jax.ShapeDtypeStruct((1, pieces[0].shape[0], sum(counts) * rows), BF16),
        compiler_params=pltpu.CompilerParams(vmem_limit_bytes=32 << 20),
        cost_estimate=COST,
        name="assemble",
    )(columns, *pieces)


def parts_of(packed, width):
    state = packed[:, :width, :].astype(F32)
    high = packed[:, width : width + 1, :].astype(F32)
    low = packed[:, width + EXTRA // 2 : width + EXTRA // 2 + 1, :].astype(F32)
    return state, high + low


def body(n, pipes, cotangent, input_map, output_map, log_decay, flight_starts, skip_gain, in_weight):
    cot, weight = cotangent[0], in_weight[0]
    writes, reads, decay = input_map[0], output_map[0], log_decay[0]
    tokens, heads = decay.shape
    width = writes.shape[1]
    size = cot.shape[1] // heads
    rows = weight.shape[0]
    m = n // 2
    mine = lax.axis_index("seq")
    slab, side = mine // 2, mine % 2
    first = side == 0

    pair = [(s, s ^ 1) for s in range(n)]

    def swap(x):
        return lax.ppermute(x, "seq", pair)

    def down(k):
        return [(s, s - 2) for s in range(2, n - 2 * (k - 1))]

    blocks = {(0, 0): weight}
    for k in range(1, m):
        blocks[1, k] = lax.ppermute(
            blocks.get((1, k - 1), weight), "seq",
            [(s, s + 2) for s in range(2 * (k - 1), n - 2)],
        )
        if k < m - 1:
            blocks[-1, k] = lax.ppermute(blocks.get((-1, k - 1), weight), "seq", down(k))

    writes_b, reads_b, decay_b, starts_b = [
        swap(x) for x in (writes, reads, decay, flight_starts)
    ]
    small = (writes_b, reads_b, decay_b, starts_b)
    ready_a = prepared(reads, decay, flight_starts)
    state_a = states_part(cot, ready_a)
    cot_b = swap(gate(cot, state_a))
    (near_a,) = near_part([gate(cot, state_a)], writes, reads, skip_gain, ready_a, False)
    ready_b = prepared(reads_b, decay_b, starts_b)
    half = heads // 2
    leaving = lax.dynamic_slice_in_dim(state_a, (1 - side) * half, half, 0)
    got = swap(gate(leaving, *small))
    kept = lax.dynamic_slice_in_dim(state_a, side * half, half, 0)
    state_0, keep_0 = parts_of(jnp.where(first, kept, got), width)
    state_1, keep_1 = parts_of(jnp.where(first, got, kept), width)
    slab_state, slab_keep = state_0 + keep_0 * state_1, keep_0 * keep_1
    later = jnp.zeros((half, width, size), BF16)
    for at in reversed(range(1, m)):
        leaving = (slab_state + slab_keep * later.astype(F32)).astype(BF16)
        if at == m - 1:
            leaving = gate(leaving, blocks[1, 1], blocks[-1, 1], ready_b[0], near_a)
        later = later + lax.ppermute(
            leaving, "seq", [(2 * at + y, 2 * at - 2 + y) for y in range(2)]
        )
    blocks[-1, m - 1] = lax.ppermute(gate(blocks[-1, m - 2], later), "seq", down(m - 1))
    other = swap(later)
    cot_b = gate(cot_b, later)
    near_b, state_b = near_part([cot_b], writes_b, reads_b, skip_gain, ready_b, True)
    last = jnp.where(first, jnp.stack([later, other]), jnp.stack([other, later]))
    last = last.reshape(heads, width, size)
    state_1, keep_1 = parts_of(jnp.where(first, state_b, state_a), width)
    early = (state_1 + keep_1 * last.astype(F32)).astype(BF16)
    later_a = jnp.where(first, early, last)
    later_b = jnp.where(first, last, early)

    plan = arrivals(m)
    slots = [[plan[q][slot] for q in range(m)] for slot in range(m)]
    count = min(m - 1, SLOTS)
    x, own, swapped = main_part(
        (near_a, near_b), (writes, writes_b), (ready_a[0], ready_b[0]), (later_a, later_b),
        weight, blocks, slots[1:count], slab, heads,
    )
    todo = [(slots[:count], (own, swapped))]
    for slot in range(count, m):
        todo.append(([slots[slot]], product(x, blocks, slots[slot], slab, tokens)))
    pieces, columns = [], []
    for picked, got in todo:
        table = jnp.array(
            [[2 * (q - way * k) for q, (way, k) in enumerate(picks)] for picks in picked],
            jnp.int32,
        )[:, slab]
        for flip in range(2):
            route = [
                (s * pipes + p, (s ^ flip) * pipes + (p - 1) % pipes)
                for s in range(n) for p in range(pipes)
            ]
            pieces.append(lax.ppermute(got[flip], ("seq", "pipe"), route))
            columns.append(table + (side ^ flip))
    return assembled(pieces, jnp.concatenate(columns), rows)


def solution(mesh):
    n, pipes = mesh.shape["seq"], mesh.shape["pipe"]
    placed = (
        P("pipe", "seq", None),
        P("pipe", "seq", None),
        P("pipe", "seq", None),
        P("pipe", "seq", None),
        P("pipe", "seq"),
        P("pipe", None),
        P("pipe", "seq", None),
    )
    return jax.shard_map(
        functools.partial(body, n, pipes),
        mesh=mesh,
        in_specs=placed,
        out_specs=P("pipe", "seq", None),
        check_vma=False,
    )
```

```python
import functools

import jax
import jax.numpy as jnp
from jax import lax
from jax.experimental import pallas as pl
from jax.experimental.pallas import tpu as pltpu
from jax.sharding import PartitionSpec as P

CHUNK = 128
GROUP = 4
EXTRA = 16
BF16 = jnp.bfloat16
F32 = jnp.float32
COST = pl.CostEstimate(flops=0, bytes_accessed=0, transcendentals=0)


def turned(cols_ref, first):
    lanes = cols_ref.shape[1]
    return pltpu.roll(
        cols_ref[...], lax.rem(2 * lanes - first - GROUP * pl.program_id(0), lanes), axis=1
    )


def prep_kernel(
    chunks, heads, ext_ref, reads_ref,
    cols_ref, cumr_ref, openr_ref, keep_ref, whole_ref, cntr_ref, readst_ref, allr_ref,
):
    groups = heads // GROUP
    rows = heads + 8
    col = lax.broadcasted_iota(jnp.int32, (rows, CHUNK), 1)
    after = jnp.zeros((rows, 1), F32)
    kept = []
    for c in reversed(range(chunks)):
        at = slice(c * CHUNK, (c + 1) * CHUNK)
        cum = ext_ref[:, at]
        shift = 1
        while shift < CHUNK:
            cum = cum + jnp.where(col >= shift, pltpu.roll(cum, shift, axis=1), 0.0)
            shift *= 2
        last = cum[:, CHUNK - 1 :]
        cnt, end = cum[heads : heads + 1], last[heads : heads + 1]
        linked = jnp.where(cnt == end, 1.0, 0.0)
        tail = jnp.exp(jnp.minimum(last - cum, 0.0)) * linked
        later = jnp.where(after[heads : heads + 1] == 0.0, jnp.exp(after), 0.0)
        reach = tail * later
        opened = jnp.exp(cum) * jnp.where(cnt == 0.0, 1.0, 0.0)
        keep = jnp.where(end == 0.0, jnp.exp(last), 0.0)
        after = after + last
        kept.append((cum, last))
        cntr_ref[:, at] = cnt
        stack = [cum, tail[:heads], reach[:heads]]
        stack.append(jnp.zeros((CHUNK - 3 * heads - 8, CHUNK), F32))
        cols_ref[at, :] = jnp.concatenate(stack, axis=0).T
        for g in range(groups):
            lane = slice(g * GROUP, (g + 1) * GROUP)
            cumr_ref[g, :, at] = cum[lane]
            openr_ref[g, :, at] = opened[lane]
            keep_ref[g, c * GROUP : (c + 1) * GROUP, :] = jnp.broadcast_to(
                keep[lane], (GROUP, 128)
            )
    whole = jnp.where(after[heads : heads + 1] == 0.0, jnp.exp(after), 0.0)
    for g in range(groups):
        whole_ref[g] = jnp.broadcast_to(whole[g * GROUP : (g + 1) * GROUP], (GROUP, 128))
    before = jnp.zeros((rows, 1), F32)
    for c, (cum, last) in enumerate(reversed(kept)):
        total = cum + before
        opened = jnp.exp(total) * jnp.where(total[heads : heads + 1] == 0.0, 1.0, 0.0)
        before = before + last
        for g in range(groups):
            allr_ref[g, :, c * CHUNK : (c + 1) * CHUNK] = opened[g * GROUP : (g + 1) * GROUP]
    readst_ref[...] = reads_ref[...].astype(F32).T.astype(BF16)


def near_kernel(
    chunks, heads, pieces, gain_ref, writes_ref, reads_ref, readst_ref, cntr_ref, cols_ref,
    cumr_ref, openr_ref, keep_ref, whole_ref, *refs,
):
    cot_refs, out_ref, score_ref = refs[: len(pieces)], refs[len(pieces)], refs[-1]
    state_ref = refs[-2] if len(refs) > len(pieces) + 2 else None
    group = pl.program_id(0)

    @pl.when(group == 0)
    def _():
        row = lax.broadcasted_iota(jnp.int32, (CHUNK, CHUNK), 0)
        col = lax.broadcasted_iota(jnp.int32, (CHUNK, CHUNK), 1)
        for c in range(chunks):
            at = slice(c * CHUNK, (c + 1) * CHUNK)
            scores = lax.dot_general(
                writes_ref[at, :], reads_ref[at, :], (((1,), (1,)), ((), ())),
                preferred_element_type=F32,
            )
            linked = (row <= col) & (cols_ref[at, heads : heads + 1] == cntr_ref[:, at])
            score_ref[at, :] = jnp.where(linked, scores, 0.0)

    cols = turned(cols_ref, 0)
    where = []
    for p, length in enumerate(pieces):
        where += [(p, i) for i in range(length // CHUNK)]
    width = readst_ref.shape[0]
    for j in range(GROUP):
        lane = slice(j * 128, (j + 1) * 128)
        gain = gain_ref[0, group * GROUP + j]
        later = None
        for c in reversed(range(chunks)):
            at = slice(c * CHUNK, (c + 1) * CHUNK)
            piece, inner = where[c]
            cot = cot_refs[piece][inner * CHUNK : (inner + 1) * CHUNK, lane]
            spread = cumr_ref[0, j : j + 1, at] - cols[at, j : j + 1]
            weight = (jnp.exp(jnp.minimum(spread, 0.0)) * score_ref[at, :]).astype(BF16)
            if later is None:
                total = jnp.dot(weight, cot, preferred_element_type=F32)
            else:
                tail = cols[at, heads + 8 + j : heads + 9 + j]
                reach = (tail * writes_ref[at, :].astype(F32)).astype(BF16)
                total = jnp.dot(
                    jnp.concatenate([weight, reach], axis=1),
                    jnp.concatenate([cot, later.astype(BF16)], axis=0),
                    preferred_element_type=F32,
                )
            out_ref[at, lane] = (total + gain * cot.astype(F32)).astype(BF16)
            if c == 0 and state_ref is None:
                continue
            scaled = (readst_ref[:, at].astype(F32) * openr_ref[0, j : j + 1, at]).astype(BF16)
            state = jnp.dot(scaled, cot, preferred_element_type=F32)
            if later is not None:
                state = state + keep_ref[0, c * GROUP + j : c * GROUP + j + 1, :] * later
            later = state
        if state_ref is not None:
            pack(state_ref, j, later, whole_ref[0, j : j + 1, :])


def pack(state_ref, j, state, keep):
    width = state.shape[0]
    state_ref[j, :width, :] = state.astype(BF16)
    keep = jnp.broadcast_to(keep, (EXTRA, 128))
    high = keep.astype(BF16)
    low = (keep - high.astype(F32)).astype(BF16)
    top = lax.broadcasted_iota(jnp.int32, (EXTRA, 128), 0) < EXTRA // 2
    state_ref[j, width:, :] = jnp.where(top, high.astype(F32), low.astype(F32)).astype(BF16)


def states_kernel(readst_ref, allr_ref, whole_ref, cot_ref, state_ref):
    for j in range(GROUP):
        scaled = (readst_ref[...].astype(F32) * allr_ref[0, j : j + 1, :]).astype(BF16)
        state = jnp.dot(scaled, cot_ref[:, j * 128 : (j + 1) * 128], preferred_element_type=F32)
        pack(state_ref, j, state, whole_ref[0, j : j + 1, :])


def fetch(slab_ref, which, blocks, held, sem):
    for b, block in enumerate(blocks):
        chosen = [slab_ref[0] == q for q, w in enumerate(which) if w == b]
        if chosen:

            @pl.when(functools.reduce(jnp.logical_or, chosen))
            def _():
                pltpu.make_async_copy(block, held, sem).start()


def far_kernel(heads, *refs):
    near, writes, cols, later, x_ref = refs[0:2], refs[2:4], refs[4:6], refs[6:8], refs[8]
    tokens, step_width = near[0].shape
    step = pl.program_id(0)
    for side in range(2):
        reach = turned(cols[side], 2 * heads + 8)
        for j in range(GROUP):
            lane = slice(j * 128, (j + 1) * 128)
            at = pl.ds(pl.multiple_of(step * step_width + j * 128, 128), 128)
            far = jnp.dot(writes[side][...], later[side][j], preferred_element_type=F32)
            total = near[side][:, lane].astype(F32) + reach[:, j : j + 1] * far
            x_ref[side * tokens : (side + 1) * tokens, at] = total.astype(BF16)


def product_kernel(which, slab_ref, x_ref, *refs):
    blocks, (own_ref, other_ref, held, sem) = refs[:-4], refs[-4:]
    fetch(slab_ref, which, blocks, held, sem)
    pltpu.make_async_copy(blocks[0], held, sem).wait()
    tokens = own_ref.shape[0]
    for side, out_ref in enumerate((own_ref, other_ref)):
        out_ref[...] = lax.dot_general(
            x_ref[side * tokens : (side + 1) * tokens, :], held[...],
            (((1,), (1,)), ((), ())), preferred_element_type=F32,
        ).astype(BF16)


def gate(x, *after):
    return lax.optimization_barrier((x,) + after)[0]


def step3(g, *_):
    return (g, 0, 0)


def whole2(g, *_):
    return (0, 0)


def columns2(g, *_):
    return (0, g)


def prepared(reads, ext):
    heads = ext.shape[0] - 8
    tokens, width = reads.shape
    chunks = tokens // CHUNK
    groups = heads // GROUP

    def like(*shape):
        return jax.ShapeDtypeStruct(shape, F32)

    return pl.pallas_call(
        functools.partial(prep_kernel, chunks, heads),
        out_shape=[like(tokens, CHUNK)]
        + [like(groups, GROUP, tokens)] * 2
        + [like(groups, chunks * GROUP, 128), like(groups, GROUP, 128), like(1, tokens)]
        + [jax.ShapeDtypeStruct((width, tokens), BF16), like(groups, GROUP, tokens)],
        cost_estimate=COST,
        name="prep",
    )(ext, reads)


def near_part(cots, writes, reads, gains, ready, states):
    cols, cumr, openr, keep, whole, cntr, reads_t = ready[:7]
    heads = gains.shape[1]
    tokens, width = writes.shape
    size = cots[0].shape[1] // heads
    chunks = tokens // CHUNK
    groups = heads // GROUP
    pieces = [c.shape[0] for c in cots]
    return pl.pallas_call(
        functools.partial(near_kernel, chunks, heads, pieces),
        grid=(groups,),
        in_specs=[
            pl.BlockSpec(memory_space=pltpu.SMEM),
            pl.BlockSpec((tokens, width), whole2),
            pl.BlockSpec((tokens, width), whole2),
            pl.BlockSpec((width, tokens), whole2),
            pl.BlockSpec((1, tokens), whole2),
            pl.BlockSpec((tokens, CHUNK), whole2),
            pl.BlockSpec((1, GROUP, tokens), step3),
            pl.BlockSpec((1, GROUP, tokens), step3),
            pl.BlockSpec((1, chunks * GROUP, 128), step3),
            pl.BlockSpec((1, GROUP, 128), step3),
        ]
        + [pl.BlockSpec((length, GROUP * size), columns2) for length in pieces],
        out_specs=[
            pl.BlockSpec((tokens, GROUP * size), columns2),
            pl.BlockSpec((GROUP, width + EXTRA, size), step3),
        ][: 1 + states],
        out_shape=[
            jax.ShapeDtypeStruct((tokens, heads * size), BF16),
            jax.ShapeDtypeStruct((heads, width + EXTRA, size), BF16),
        ][: 1 + states],
        scratch_shapes=[pltpu.VMEM((tokens, CHUNK), F32)],
        cost_estimate=COST,
        name="near",
    )(gains, writes, reads, reads_t, cntr, cols, cumr, openr, keep, whole, *cots)


def states_part(cot, ready):
    whole, reads_t, allr = ready[4], ready[6], ready[7]
    groups, _, tokens = allr.shape
    width = reads_t.shape[0]
    heads = groups * GROUP
    size = cot.shape[1] // heads
    return pl.pallas_call(
        states_kernel,
        grid=(groups,),
        in_specs=[
            pl.BlockSpec((width, tokens), whole2),
            pl.BlockSpec((1, GROUP, tokens), step3),
            pl.BlockSpec((1, GROUP, 128), step3),
            pl.BlockSpec((tokens, GROUP * size), columns2),
        ],
        out_specs=pl.BlockSpec((GROUP, width + EXTRA, size), step3),
        out_shape=jax.ShapeDtypeStruct((heads, width + EXTRA, size), BF16),
        cost_estimate=COST,
        name="states",
    )(reads_t, allr, whole, cot)


def arrivals(m):
    plan = []
    for q in range(m):
        order = [(0, 0)]
        for k in range(1, m):
            order += [(1, k)] * (q >= k) + [(-1, k)] * (q + k < m)
        plan.append(order)
    return plan


def indexed(slots):
    distinct = []
    for picks in slots:
        distinct += [p for p in picks if p not in distinct]
    return distinct, [[distinct.index(p) for p in picks] for picks in slots]


def far_part(near, writes, cols, later, heads):
    tokens, width = writes[0].shape
    depth = near[0].shape[1]
    size = depth // heads
    return pl.pallas_call(
        functools.partial(far_kernel, heads),
        grid=(heads // GROUP,),
        in_specs=[pl.BlockSpec((tokens, GROUP * size), columns2)] * 2
        + [pl.BlockSpec((tokens, width), whole2)] * 2
        + [pl.BlockSpec((tokens, CHUNK), whole2)] * 2
        + [pl.BlockSpec((GROUP, width, size), step3)] * 2,
        out_specs=pl.BlockSpec(memory_space=pltpu.VMEM),
        out_shape=pltpu.VMEM((2 * tokens, depth), BF16),
        compiler_params=pltpu.CompilerParams(vmem_limit_bytes=36 << 20),
        cost_estimate=COST,
        name="far",
    )(*near, *writes, *cols, *later)


def product(x, blocks, picks, slab, tokens):
    distinct, (which,) = indexed([picks])
    rows, depth = blocks[picks[0]].shape
    vmem = pl.BlockSpec(memory_space=pltpu.VMEM)
    return pl.pallas_call(
        functools.partial(product_kernel, which),
        in_specs=[pl.BlockSpec(memory_space=pltpu.SMEM), vmem]
        + [pl.BlockSpec(memory_space=pl.ANY)] * len(distinct),
        out_specs=[vmem] * 2,
        scratch_shapes=[
            pltpu.VMEM((rows, depth), BF16),
            pltpu.SemaphoreType.DMA,
        ],
        out_shape=[jax.ShapeDtypeStruct((tokens, rows), BF16)] * 2,
        compiler_params=pltpu.CompilerParams(vmem_limit_bytes=24 << 20),
        cost_estimate=COST,
        name="product",
    )(slab.reshape(1), x, *[blocks[p] for p in distinct])


def assemble_kernel(counts, mine_ref, columns_ref, *refs):
    pieces, out_ref = refs[:-1], refs[-1]
    rows = pieces[0].shape[1] // counts[0]
    at = 0
    for piece, count in zip(pieces, counts):
        for i in range(count):
            column = pl.multiple_of(columns_ref[mine_ref[0], at] * rows, rows)
            out_ref[0, :, pl.ds(column, rows)] = piece[:, i * rows : (i + 1) * rows]
            at += 1


def assembled(pieces, columns, mine, rows):
    counts = [piece.shape[1] // rows for piece in pieces]
    if rows % 128:
        result = jnp.zeros((1, pieces[0].shape[0], sum(counts) * rows), BF16)
        at = 0
        for piece, count in zip(pieces, counts):
            for i in range(count):
                result = lax.dynamic_update_slice(
                    result, piece[None, :, i * rows : (i + 1) * rows], (0, 0, columns[mine, at] * rows)
                )
                at += 1
        return result
    vmem = pl.BlockSpec(memory_space=pltpu.VMEM)
    return pl.pallas_call(
        functools.partial(assemble_kernel, counts),
        in_specs=[pl.BlockSpec(memory_space=pltpu.SMEM)] * 2 + [vmem] * len(pieces),
        out_specs=vmem,
        out_shape=jax.ShapeDtypeStruct((1, pieces[0].shape[0], sum(counts) * rows), BF16),
        compiler_params=pltpu.CompilerParams(vmem_limit_bytes=32 << 20),
        cost_estimate=COST,
        name="assemble",
    )(mine.reshape(1), columns, *pieces)


def parts_of(packed, width):
    state = packed[:, :width, :].astype(F32)
    high = packed[:, width : width + 1, :].astype(F32)
    low = packed[:, width + EXTRA // 2 : width + EXTRA // 2 + 1, :].astype(F32)
    return state, high + low


def body(n, pipes, cotangent, input_map, output_map, log_decay, flight_starts, skip_gain, in_weight):
    cot, weight = cotangent[0], in_weight[0]
    writes, reads, decay = input_map[0], output_map[0], log_decay[0]
    tokens, heads = decay.shape
    width = writes.shape[1]
    size = cot.shape[1] // heads
    rows = weight.shape[0]
    m = n // 2
    mine = lax.axis_index("seq")
    slab, side = mine // 2, mine % 2
    first = side == 0

    pair = [(s, s ^ 1) for s in range(n)]

    def swap(x):
        return lax.ppermute(x, "seq", pair)

    def down(k):
        return [(s, s - 2) for s in range(2, n - 2 * (k - 1))]

    blocks = {(0, 0): weight}
    for k in range(1, m):
        blocks[1, k] = lax.ppermute(
            blocks.get((1, k - 1), weight), "seq",
            [(s, s + 2) for s in range(2 * (k - 1), n - 2)],
        )
        if k < m - 1:
            blocks[-1, k] = lax.ppermute(blocks.get((-1, k - 1), weight), "seq", down(k))

    starts = jnp.broadcast_to(flight_starts.astype(F32), (8, tokens))
    ext = jnp.concatenate([decay.T, starts], axis=0)
    small = writes_b, reads_b, ext_b = [swap(x) for x in (writes, reads, ext)]
    ready_a = prepared(reads, ext)
    state_a = states_part(cot, ready_a)
    cot_b = swap(gate(cot, state_a))
    (near_a,) = near_part([gate(cot, state_a)], writes, reads, skip_gain, ready_a, False)
    ready_b = prepared(reads_b, ext_b)
    half = heads // 2
    leaving = lax.dynamic_slice_in_dim(state_a, (1 - side) * half, half, 0)
    got = swap(gate(leaving, *small))
    kept = lax.dynamic_slice_in_dim(state_a, side * half, half, 0)
    state_0, keep_0 = parts_of(jnp.where(first, kept, got), width)
    state_1, keep_1 = parts_of(jnp.where(first, got, kept), width)
    slab_state, slab_keep = state_0 + keep_0 * state_1, keep_0 * keep_1
    later = jnp.zeros((half, width, size), BF16)
    for at in reversed(range(1, m)):
        leaving = (slab_state + slab_keep * later.astype(F32)).astype(BF16)
        if at == m - 1:
            leaving = gate(leaving, blocks[1, 1], blocks[-1, 1], ready_b[0], near_a)
        later = later + lax.ppermute(
            leaving, "seq", [(2 * at + y, 2 * at - 2 + y) for y in range(2)]
        )
    blocks[-1, m - 1] = lax.ppermute(gate(blocks[-1, m - 2], later), "seq", down(m - 1))
    other = swap(later)
    cot_b = gate(cot_b, later)
    near_b, state_b = near_part([cot_b], writes_b, reads_b, skip_gain, ready_b, True)
    last = jnp.where(first, jnp.stack([later, other]), jnp.stack([other, later]))
    last = last.reshape(heads, width, size)
    state_1, keep_1 = parts_of(jnp.where(first, state_b, state_a), width)
    early = (state_1 + keep_1 * last.astype(F32)).astype(BF16)
    later_a = jnp.where(first, early, last)
    later_b = jnp.where(first, last, early)

    plan = arrivals(m)
    slots = [[plan[q][slot] for q in range(m)] for slot in range(m)]
    x = far_part(
        (near_a, near_b), (writes, writes_b), (ready_a[0], ready_b[0]), (later_a, later_b), heads
    )
    todo = [([picks], product(x, blocks, picks, slab, tokens)) for picks in slots]
    pieces, columns = [], [[] for _ in range(n)]
    for picked, got in todo:
        for flip in (1, 0):
            route = [
                (s * pipes + p, (s ^ flip) * pipes + (p - 1) % pipes)
                for s in range(n) for p in range(pipes)
            ]
            pieces.append(lax.ppermute(got[flip], ("seq", "pipe"), route))
            for picks in picked:
                for s in range(n):
                    way, k = picks[s // 2]
                    columns[s].append(2 * (s // 2 - way * k) + (s % 2 ^ flip))
    return assembled(pieces, jnp.array(columns, jnp.int32), mine, rows)


def solution(mesh):
    n, pipes = mesh.shape["seq"], mesh.shape["pipe"]
    placed = (
        P("pipe", "seq", None),
        P("pipe", "seq", None),
        P("pipe", "seq", None),
        P("pipe", "seq", None),
        P("pipe", "seq"),
        P("pipe", None),
        P("pipe", "seq", None),
    )
    return jax.shard_map(
        functools.partial(body, n, pipes),
        mesh=mesh,
        in_specs=placed,
        out_specs=P("pipe", "seq", None),
        check_vma=False,
    )
```

```python
import functools

import jax
import jax.numpy as jnp
from jax import lax
from jax.experimental import pallas as pl
from jax.experimental.pallas import tpu as pltpu
from jax.sharding import PartitionSpec as P

CHUNK = 128
GROUP = 4
EXTRA = 16
BF16 = jnp.bfloat16
F32 = jnp.float32
COST = pl.CostEstimate(flops=0, bytes_accessed=0, transcendentals=0)


def turned(cols_ref, first):
    lanes = cols_ref.shape[1]
    return pltpu.roll(
        cols_ref[...], lax.rem(2 * lanes - first - GROUP * pl.program_id(0), lanes), axis=1
    )


def prep_kernel(
    chunks, heads, ext_ref, reads_ref,
    cols_ref, cumr_ref, openr_ref, keep_ref, whole_ref, cntr_ref, readst_ref, allr_ref,
):
    groups = heads // GROUP
    rows = heads + 8
    col = lax.broadcasted_iota(jnp.int32, (rows, CHUNK), 1)
    after = jnp.zeros((rows, 1), F32)
    kept = []
    for c in reversed(range(chunks)):
        at = slice(c * CHUNK, (c + 1) * CHUNK)
        cum = ext_ref[:, at]
        shift = 1
        while shift < CHUNK:
            cum = cum + jnp.where(col >= shift, pltpu.roll(cum, shift, axis=1), 0.0)
            shift *= 2
        last = cum[:, CHUNK - 1 :]
        cnt, end = cum[heads : heads + 1], last[heads : heads + 1]
        linked = jnp.where(cnt == end, 1.0, 0.0)
        tail = jnp.exp(jnp.minimum(last - cum, 0.0)) * linked
        later = jnp.where(after[heads : heads + 1] == 0.0, jnp.exp(after), 0.0)
        reach = tail * later
        opened = jnp.exp(cum) * jnp.where(cnt == 0.0, 1.0, 0.0)
        keep = jnp.where(end == 0.0, jnp.exp(last), 0.0)
        after = after + last
        kept.append((cum, last))
        cntr_ref[:, at] = cnt
        stack = [cum, tail[:heads], reach[:heads]]
        stack.append(jnp.zeros((CHUNK - 3 * heads - 8, CHUNK), F32))
        cols_ref[at, :] = jnp.concatenate(stack, axis=0).T
        for g in range(groups):
            lane = slice(g * GROUP, (g + 1) * GROUP)
            cumr_ref[g, :, at] = cum[lane]
            openr_ref[g, :, at] = opened[lane]
            keep_ref[g, c * GROUP : (c + 1) * GROUP, :] = jnp.broadcast_to(
                keep[lane], (GROUP, 128)
            )
    whole = jnp.where(after[heads : heads + 1] == 0.0, jnp.exp(after), 0.0)
    for g in range(groups):
        whole_ref[g] = jnp.broadcast_to(whole[g * GROUP : (g + 1) * GROUP], (GROUP, 128))
    before = jnp.zeros((rows, 1), F32)
    for c, (cum, last) in enumerate(reversed(kept)):
        total = cum + before
        opened = jnp.exp(total) * jnp.where(total[heads : heads + 1] == 0.0, 1.0, 0.0)
        before = before + last
        for g in range(groups):
            allr_ref[g, :, c * CHUNK : (c + 1) * CHUNK] = opened[g * GROUP : (g + 1) * GROUP]
    readst_ref[...] = reads_ref[...].astype(F32).T.astype(BF16)


def near_kernel(
    chunks, heads, pieces, gain_ref, writes_ref, reads_ref, readst_ref, cntr_ref, cols_ref,
    cumr_ref, openr_ref, keep_ref, whole_ref, *refs,
):
    cot_refs, out_ref, score_ref = refs[: len(pieces)], refs[len(pieces)], refs[-1]
    state_ref = refs[-2] if len(refs) > len(pieces) + 2 else None
    group = pl.program_id(0)

    @pl.when(group == 0)
    def _():
        row = lax.broadcasted_iota(jnp.int32, (CHUNK, CHUNK), 0)
        col = lax.broadcasted_iota(jnp.int32, (CHUNK, CHUNK), 1)
        for c in range(chunks):
            at = slice(c * CHUNK, (c + 1) * CHUNK)
            scores = lax.dot_general(
                writes_ref[at, :], reads_ref[at, :], (((1,), (1,)), ((), ())),
                preferred_element_type=F32,
            )
            linked = (row <= col) & (cols_ref[at, heads : heads + 1] == cntr_ref[:, at])
            score_ref[at, :] = jnp.where(linked, scores, 0.0)

    cols = turned(cols_ref, 0)
    where = []
    for p, length in enumerate(pieces):
        where += [(p, i) for i in range(length // CHUNK)]
    width = readst_ref.shape[0]
    for j in range(GROUP):
        lane = slice(j * 128, (j + 1) * 128)
        gain = gain_ref[0, group * GROUP + j]
        later = None
        for c in reversed(range(chunks)):
            at = slice(c * CHUNK, (c + 1) * CHUNK)
            piece, inner = where[c]
            cot = cot_refs[piece][inner * CHUNK : (inner + 1) * CHUNK, lane]
            spread = cumr_ref[0, j : j + 1, at] - cols[at, j : j + 1]
            weight = (jnp.exp(jnp.minimum(spread, 0.0)) * score_ref[at, :]).astype(BF16)
            if later is None:
                total = jnp.dot(weight, cot, preferred_element_type=F32)
            else:
                tail = cols[at, heads + 8 + j : heads + 9 + j]
                reach = (tail * writes_ref[at, :].astype(F32)).astype(BF16)
                total = jnp.dot(
                    jnp.concatenate([weight, reach], axis=1),
                    jnp.concatenate([cot, later.astype(BF16)], axis=0),
                    preferred_element_type=F32,
                )
            out_ref[at, lane] = (total + gain * cot.astype(F32)).astype(BF16)
            if c == 0 and state_ref is None:
                continue
            scaled = (readst_ref[:, at].astype(F32) * openr_ref[0, j : j + 1, at]).astype(BF16)
            state = jnp.dot(scaled, cot, preferred_element_type=F32)
            if later is not None:
                state = state + keep_ref[0, c * GROUP + j : c * GROUP + j + 1, :] * later
            later = state
        if state_ref is not None:
            pack(state_ref, j, later, whole_ref[0, j : j + 1, :])


def pack(state_ref, j, state, keep):
    width = state.shape[0]
    state_ref[j, :width, :] = state.astype(BF16)
    keep = jnp.broadcast_to(keep, (EXTRA, 128))
    high = keep.astype(BF16)
    low = (keep - high.astype(F32)).astype(BF16)
    top = lax.broadcasted_iota(jnp.int32, (EXTRA, 128), 0) < EXTRA // 2
    state_ref[j, width:, :] = jnp.where(top, high.astype(F32), low.astype(F32)).astype(BF16)


def states_kernel(readst_ref, allr_ref, whole_ref, cot_ref, state_ref):
    for j in range(GROUP):
        scaled = (readst_ref[...].astype(F32) * allr_ref[0, j : j + 1, :]).astype(BF16)
        state = jnp.dot(scaled, cot_ref[:, j * 128 : (j + 1) * 128], preferred_element_type=F32)
        pack(state_ref, j, state, whole_ref[0, j : j + 1, :])


def fetch(slab_ref, which, blocks, held, sem):
    for b, block in enumerate(blocks):
        chosen = [slab_ref[0] == q for q, w in enumerate(which) if w == b]
        if chosen:

            @pl.when(functools.reduce(jnp.logical_or, chosen))
            def _():
                pltpu.make_async_copy(block, held, sem).start()


def far_kernel(heads, *refs):
    near, writes, cols, later, x_ref = refs[0:2], refs[2:4], refs[4:6], refs[6:8], refs[8]
    tokens, step_width = near[0].shape
    step = pl.program_id(0)
    for side in range(2):
        reach = turned(cols[side], 2 * heads + 8)
        for j in range(GROUP):
            lane = slice(j * 128, (j + 1) * 128)
            at = pl.ds(pl.multiple_of(step * step_width + j * 128, 128), 128)
            far = jnp.dot(writes[side][...], later[side][j], preferred_element_type=F32)
            total = near[side][:, lane].astype(F32) + reach[:, j : j + 1] * far
            x_ref[side * tokens : (side + 1) * tokens, at] = total.astype(BF16)


def product_kernel(which, slab_ref, x_ref, *refs):
    blocks, (own_ref, other_ref, held, sem) = refs[:-4], refs[-4:]
    fetch(slab_ref, which, blocks, held, sem)
    pltpu.make_async_copy(blocks[0], held, sem).wait()
    tokens = own_ref.shape[0]
    for side, out_ref in enumerate((own_ref, other_ref)):
        out_ref[...] = lax.dot_general(
            x_ref[side * tokens : (side + 1) * tokens, :], held[...],
            (((1,), (1,)), ((), ())), preferred_element_type=F32,
        ).astype(BF16)


def gate(x, *after):
    return lax.optimization_barrier((x,) + after)[0]


def step3(g, *_):
    return (g, 0, 0)


def whole2(g, *_):
    return (0, 0)


def columns2(g, *_):
    return (0, g)


def prepared(reads, ext):
    heads = ext.shape[0] - 8
    tokens, width = reads.shape
    chunks = tokens // CHUNK
    groups = heads // GROUP

    def like(*shape):
        return jax.ShapeDtypeStruct(shape, F32)

    return pl.pallas_call(
        functools.partial(prep_kernel, chunks, heads),
        out_shape=[like(tokens, CHUNK)]
        + [like(groups, GROUP, tokens)] * 2
        + [like(groups, chunks * GROUP, 128), like(groups, GROUP, 128), like(1, tokens)]
        + [jax.ShapeDtypeStruct((width, tokens), BF16), like(groups, GROUP, tokens)],
        cost_estimate=COST,
        name="prep",
    )(ext, reads)


def near_part(cots, writes, reads, gains, ready, states):
    cols, cumr, openr, keep, whole, cntr, reads_t = ready[:7]
    heads = gains.shape[1]
    tokens, width = writes.shape
    size = cots[0].shape[1] // heads
    chunks = tokens // CHUNK
    groups = heads // GROUP
    pieces = [c.shape[0] for c in cots]
    return pl.pallas_call(
        functools.partial(near_kernel, chunks, heads, pieces),
        grid=(groups,),
        in_specs=[
            pl.BlockSpec(memory_space=pltpu.SMEM),
            pl.BlockSpec((tokens, width), whole2),
            pl.BlockSpec((tokens, width), whole2),
            pl.BlockSpec((width, tokens), whole2),
            pl.BlockSpec((1, tokens), whole2),
            pl.BlockSpec((tokens, CHUNK), whole2),
            pl.BlockSpec((1, GROUP, tokens), step3),
            pl.BlockSpec((1, GROUP, tokens), step3),
            pl.BlockSpec((1, chunks * GROUP, 128), step3),
            pl.BlockSpec((1, GROUP, 128), step3),
        ]
        + [pl.BlockSpec((length, GROUP * size), columns2) for length in pieces],
        out_specs=[
            pl.BlockSpec((tokens, GROUP * size), columns2),
            pl.BlockSpec((GROUP, width + EXTRA, size), step3),
        ][: 1 + states],
        out_shape=[
            jax.ShapeDtypeStruct((tokens, heads * size), BF16),
            jax.ShapeDtypeStruct((heads, width + EXTRA, size), BF16),
        ][: 1 + states],
        scratch_shapes=[pltpu.VMEM((tokens, CHUNK), F32)],
        cost_estimate=COST,
        name="near",
    )(gains, writes, reads, reads_t, cntr, cols, cumr, openr, keep, whole, *cots)


def states_part(cot, ready):
    whole, reads_t, allr = ready[4], ready[6], ready[7]
    groups, _, tokens = allr.shape
    width = reads_t.shape[0]
    heads = groups * GROUP
    size = cot.shape[1] // heads
    return pl.pallas_call(
        states_kernel,
        grid=(groups,),
        in_specs=[
            pl.BlockSpec((width, tokens), whole2),
            pl.BlockSpec((1, GROUP, tokens), step3),
            pl.BlockSpec((1, GROUP, 128), step3),
            pl.BlockSpec((tokens, GROUP * size), columns2),
        ],
        out_specs=pl.BlockSpec((GROUP, width + EXTRA, size), step3),
        out_shape=jax.ShapeDtypeStruct((heads, width + EXTRA, size), BF16),
        cost_estimate=COST,
        name="states",
    )(reads_t, allr, whole, cot)


def arrivals(m):
    plan = []
    for q in range(m):
        order = [(0, 0)]
        for k in range(1, m):
            order += [(1, k)] * (q >= k) + [(-1, k)] * (q + k < m)
        plan.append(order)
    return plan


def indexed(slots):
    distinct = []
    for picks in slots:
        distinct += [p for p in picks if p not in distinct]
    return distinct, [[distinct.index(p) for p in picks] for picks in slots]


def far_part(near, writes, cols, later, heads):
    tokens, width = writes[0].shape
    depth = near[0].shape[1]
    size = depth // heads
    return pl.pallas_call(
        functools.partial(far_kernel, heads),
        grid=(heads // GROUP,),
        in_specs=[pl.BlockSpec((tokens, GROUP * size), columns2)] * 2
        + [pl.BlockSpec((tokens, width), whole2)] * 2
        + [pl.BlockSpec((tokens, CHUNK), whole2)] * 2
        + [pl.BlockSpec((GROUP, width, size), step3)] * 2,
        out_specs=pl.BlockSpec(memory_space=pltpu.VMEM),
        out_shape=pltpu.VMEM((2 * tokens, depth), BF16),
        compiler_params=pltpu.CompilerParams(vmem_limit_bytes=36 << 20),
        cost_estimate=COST,
        name="far",
    )(*near, *writes, *cols, *later)


def product(x, blocks, picks, slab, tokens):
    distinct, (which,) = indexed([picks])
    rows, depth = blocks[picks[0]].shape
    vmem = pl.BlockSpec(memory_space=pltpu.VMEM)
    return pl.pallas_call(
        functools.partial(product_kernel, which),
        in_specs=[pl.BlockSpec(memory_space=pltpu.SMEM), vmem]
        + [pl.BlockSpec(memory_space=pl.ANY)] * len(distinct),
        out_specs=[vmem] * 2,
        scratch_shapes=[
            pltpu.VMEM((rows, depth), BF16),
            pltpu.SemaphoreType.DMA,
        ],
        out_shape=[jax.ShapeDtypeStruct((tokens, rows), BF16)] * 2,
        compiler_params=pltpu.CompilerParams(vmem_limit_bytes=24 << 20),
        cost_estimate=COST,
        name="product",
    )(slab.reshape(1), x, *[blocks[p] for p in distinct])


def assemble_kernel(counts, mine_ref, columns_ref, *refs):
    pieces, out_ref = refs[:-1], refs[-1]
    rows = pieces[0].shape[1] // counts[0]
    at = 0
    for piece, count in zip(pieces, counts):
        for i in range(count):
            column = pl.multiple_of(columns_ref[mine_ref[0], at] * rows, rows)
            out_ref[0, :, pl.ds(column, rows)] = piece[:, i * rows : (i + 1) * rows]
            at += 1


def assembled(pieces, columns, mine, rows):
    counts = [piece.shape[1] // rows for piece in pieces]
    if rows % 128:
        result = jnp.zeros((1, pieces[0].shape[0], sum(counts) * rows), BF16)
        at = 0
        for piece, count in zip(pieces, counts):
            for i in range(count):
                result = lax.dynamic_update_slice(
                    result, piece[None, :, i * rows : (i + 1) * rows], (0, 0, columns[mine, at] * rows)
                )
                at += 1
        return result
    vmem = pl.BlockSpec(memory_space=pltpu.VMEM)
    return pl.pallas_call(
        functools.partial(assemble_kernel, counts),
        in_specs=[pl.BlockSpec(memory_space=pltpu.SMEM)] * 2 + [vmem] * len(pieces),
        out_specs=vmem,
        out_shape=jax.ShapeDtypeStruct((1, pieces[0].shape[0], sum(counts) * rows), BF16),
        compiler_params=pltpu.CompilerParams(vmem_limit_bytes=32 << 20),
        cost_estimate=COST,
        name="assemble",
    )(mine.reshape(1), columns, *pieces)


def parts_of(packed, width):
    state = packed[:, :width, :].astype(F32)
    high = packed[:, width : width + 1, :].astype(F32)
    low = packed[:, width + EXTRA // 2 : width + EXTRA // 2 + 1, :].astype(F32)
    return state, high + low


def body(n, pipes, cotangent, input_map, output_map, log_decay, flight_starts, skip_gain, in_weight):
    cot, weight = cotangent[0], in_weight[0]
    writes, reads, decay = input_map[0], output_map[0], log_decay[0]
    tokens, heads = decay.shape
    width = writes.shape[1]
    size = cot.shape[1] // heads
    rows = weight.shape[0]
    m = n // 2
    mine = lax.axis_index("seq")
    slab, side = mine // 2, mine % 2
    first = side == 0

    pair = [(s, s ^ 1) for s in range(n)]

    def swap(x):
        return lax.ppermute(x, "seq", pair)

    def down(k):
        return [(s, s - 2) for s in range(2, n - 2 * (k - 1))]

    blocks = {(0, 0): weight}
    for k in range(1, m):
        blocks[1, k] = lax.ppermute(
            blocks.get((1, k - 1), weight), "seq",
            [(s, s + 2) for s in range(2 * (k - 1), n - 2)],
        )
        if k < m - 1:
            blocks[-1, k] = lax.ppermute(blocks.get((-1, k - 1), weight), "seq", down(k))

    starts = jnp.broadcast_to(flight_starts.astype(F32), (8, tokens))
    ext = jnp.concatenate([decay.T, starts], axis=0)
    small = writes_b, reads_b, ext_b = [swap(x) for x in (writes, reads, ext)]
    ready_a = prepared(reads, ext)
    state_a = states_part(cot, ready_a)
    cot_b = swap(gate(cot, state_a))
    (near_a,) = near_part([gate(cot, state_a)], writes, reads, skip_gain, ready_a, False)
    ready_b = prepared(reads_b, ext_b)
    half = heads // 2
    leaving = lax.dynamic_slice_in_dim(state_a, (1 - side) * half, half, 0)
    got = swap(gate(leaving, *small))
    kept = lax.dynamic_slice_in_dim(state_a, side * half, half, 0)
    state_0, keep_0 = parts_of(jnp.where(first, kept, got), width)
    state_1, keep_1 = parts_of(jnp.where(first, got, kept), width)
    slab_state, slab_keep = state_0 + keep_0 * state_1, keep_0 * keep_1
    later = jnp.zeros((half, width, size), BF16)
    for at in reversed(range(1, m)):
        leaving = (slab_state + slab_keep * later.astype(F32)).astype(BF16)
        if at == m - 1:
            leaving = gate(leaving, ready_b[0], near_a)
        elif at == m - 2:
            leaving = gate(leaving, blocks[1, 1], blocks[-1, 1])
        later = later + lax.ppermute(
            leaving, "seq", [(2 * at + y, 2 * at - 2 + y) for y in range(2)]
        )
    blocks[-1, m - 1] = lax.ppermute(gate(blocks[-1, m - 2], later), "seq", down(m - 1))
    other = swap(later)
    cot_b = gate(cot_b, later)
    near_b, state_b = near_part([cot_b], writes_b, reads_b, skip_gain, ready_b, True)
    other = gate(other, state_b)
    last = jnp.where(first, jnp.stack([later, other]), jnp.stack([other, later]))
    last = last.reshape(heads, width, size)
    state_1, keep_1 = parts_of(jnp.where(first, state_b, state_a), width)
    early = (state_1 + keep_1 * last.astype(F32)).astype(BF16)
    later_a = jnp.where(first, early, last)
    later_b = jnp.where(first, last, early)

    plan = arrivals(m)
    slots = [[plan[q][slot] for q in range(m)] for slot in range(m)]
    x = far_part(
        (near_a, near_b), (writes, writes_b), (ready_a[0], ready_b[0]), (later_a, later_b), heads
    )
    todo = [([picks], product(x, blocks, picks, slab, tokens)) for picks in slots]
    pieces, columns = [], [[] for _ in range(n)]
    for picked, got in todo:
        for flip in (1, 0):
            route = [
                (s * pipes + p, (s ^ flip) * pipes + (p - 1) % pipes)
                for s in range(n) for p in range(pipes)
            ]
            pieces.append(lax.ppermute(got[flip], ("seq", "pipe"), route))
            for picks in picked:
                for s in range(n):
                    way, k = picks[s // 2]
                    columns[s].append(2 * (s // 2 - way * k) + (s % 2 ^ flip))
    return assembled(pieces, jnp.array(columns, jnp.int32), mine, rows)


def solution(mesh):
    n, pipes = mesh.shape["seq"], mesh.shape["pipe"]
    placed = (
        P("pipe", "seq", None),
        P("pipe", "seq", None),
        P("pipe", "seq", None),
        P("pipe", "seq", None),
        P("pipe", "seq"),
        P("pipe", None),
        P("pipe", "seq", None),
    )
    return jax.shard_map(
        functools.partial(body, n, pipes),
        mesh=mesh,
        in_specs=placed,
        out_specs=P("pipe", "seq", None),
        check_vma=False,
    )
```
